32 devices in a mesh: ctx: 4 (over z), head: 8 (over y, x, core).
Axes of the slice: x: 2, y: 2, z: 4, core: 2. Of those that a mesh axis runs over, the one named last changes fastest.
Arguments:
- queries: bfloat16 [1024, 8192], P('ctx', 'head'), may hold values from -6 to 6
- key_vectors: bfloat16 [1024, 1024], P('ctx'), may hold values from -6 to 6
- value_head_vectors: bfloat16 [1024, 1024], P('ctx'), may hold values from -6 to 6
- block_pattern: int32 [8, 8], replicated, may hold values from 0 to 1
- out_weight: bfloat16 [8192, 8192], P(None, 'head'), may hold values from -0.625 to 0.625
Outputs:
- layer_out: bfloat16 [1024, 8192], P('ctx', 'head')
The draws below stay inside these ranges and needn't reach their ends.
All inputs are finite; a program needn't handle non-finite values.
Results may differ from the reference program's by a relative error of at most 0.013.
Values may be sent and summed in bfloat16 or wider, within the bound.
No kernel may reach another device: no remote copies, remote signals or barrier semaphores. Data moves between devices by JAX's collectives and lax.ppermute only.
A program may use at most 64 MiB of HBM per device.

```python
import math
import jax
import jax.numpy as jnp
from jax import lax

D = 8192
QUERY_HEADS = 64
KEY_VALUE_HEADS = 8
HEAD_SIZE = 128
BLOCK = 128
SEQUENCE_TOKENS = 1024
NBLK = 8


def draw_queries(key, part):
    complete_shape = (SEQUENCE_TOKENS, KEY_VALUE_HEADS, QUERY_HEADS // KEY_VALUE_HEADS, HEAD_SIZE)
    base_offset = jax.random.truncated_normal(jax.random.fold_in(key, 1), -4.0, 4.0, complete_shape, jnp.float32)
    return base_offset.reshape(SEQUENCE_TOKENS, QUERY_HEADS * HEAD_SIZE).astype(jnp.bfloat16)


def draw_key_vectors(key, part):
    complete_shape = (SEQUENCE_TOKENS, KEY_VALUE_HEADS, HEAD_SIZE)
    base_offset = jax.random.truncated_normal(jax.random.fold_in(key, 2), -4.0, 4.0, complete_shape, jnp.float32)
    return base_offset.reshape(SEQUENCE_TOKENS, KEY_VALUE_HEADS * HEAD_SIZE).astype(jnp.bfloat16)


def draw_block_pattern(key, part):
    density = jax.random.randint(jax.random.fold_in(key, 3), (NBLK, 1), 1, 8)
    raw_levels = jax.random.randint(jax.random.fold_in(key, 4), (NBLK, NBLK), 0, 8)
    return (raw_levels < density).astype(jnp.int32)


def shard_levels(key, dims, shards, smallest, high):
    def one(dim, blocks):
        draws = jax.random.uniform(jax.random.fold_in(jax.random.fold_in(key, 6), dim), (blocks,), jnp.float32, smallest / len(shards), high / len(shards))
        return jnp.repeat(jnp.exp(draws), dims[dim] // blocks).reshape((-1,) + (1,) * (len(dims) - dim - 1))

    factor_of = one(*shards[0])
    for cut in shards[1:]:
        factor_of = factor_of * one(*cut)
    return factor_of


def noise(own_key, shape, scale, bound, shards=(), held_as=jnp.bfloat16):
    values = scale * jax.random.normal(own_key, shape, jnp.float32)
    if shards:
        values = values * shard_levels(own_key, shape, shards, -0.22, 0.18)
    return jnp.clip(values, -bound, bound).astype(held_as)


def setup_inputs(seed: int = 0) -> dict:
    arg_keys = jax.random.split(jax.random.key(seed), 6)
    return {
        "queries": draw_queries(jax.random.fold_in(arg_keys[5], 71), 0),
        "key_vectors": draw_key_vectors(jax.random.fold_in(arg_keys[5], 71), 0),
        "value_head_vectors": noise(arg_keys[2], (SEQUENCE_TOKENS, KEY_VALUE_HEADS * HEAD_SIZE), 1.0, 6.0, ((0, 4),)),
        "block_pattern": draw_block_pattern(jax.random.fold_in(arg_keys[5], 71), 0),
        "out_weight": noise(arg_keys[4], (QUERY_HEADS * HEAD_SIZE, D), 0.04, 0.625, ((1, 8),)),
    }


def reference(queries, key_vectors, value_head_vectors, block_pattern, out_weight):
    block_total = block_pattern.shape[0]
    seq_tokens = queries.shape[0]
    block_ids = jnp.arange(block_total, dtype=jnp.int32)
    active = (block_pattern == 1) | (block_ids[:, None] == block_ids[None, :])
    token_mask = jnp.repeat(jnp.repeat(active, BLOCK, axis=0), BLOCK, axis=1)
    query_group_count = QUERY_HEADS // KEY_VALUE_HEADS
    score_scale = 1.0 / math.sqrt(HEAD_SIZE)

    def single_head(head_index):
        key_head = head_index // query_group_count
        query_part = lax.dynamic_slice_in_dim(queries, head_index * HEAD_SIZE, HEAD_SIZE, 1)
        key_part = lax.dynamic_slice_in_dim(key_vectors, key_head * HEAD_SIZE, HEAD_SIZE, 1)
        value_part = lax.dynamic_slice_in_dim(value_head_vectors, key_head * HEAD_SIZE, HEAD_SIZE, 1)
        scores = jnp.dot(query_part, key_part.T, preferred_element_type=jnp.float32) * score_scale
        scores = jnp.where(token_mask, scores, -jnp.inf)
        row_top = lax.optimization_barrier(jnp.max(scores, axis=1, keepdims=True))
        weights = jnp.exp(scores - row_top)
        total = lax.optimization_barrier(jnp.sum(weights, axis=1, keepdims=True))
        summed = jnp.dot(weights.astype(jnp.bfloat16), value_part, preferred_element_type=jnp.float32)
        return summed / total
    heads_out = lax.map(single_head, jnp.arange(QUERY_HEADS, dtype=jnp.int32))
    attended = jnp.transpose(heads_out, (1, 0, 2)).reshape(seq_tokens, QUERY_HEADS * HEAD_SIZE).astype(jnp.bfloat16)
    return jnp.dot(attended, out_weight, preferred_element_type=jnp.float32).astype(jnp.bfloat16)
```

```python
import functools
import math

import jax
import jax.numpy as jnp
from jax import lax
from jax.experimental import pallas as pl
from jax.experimental.pallas import tpu as pltpu
from jax.sharding import PartitionSpec as P

QUERY_HEADS = 64
KEY_VALUE_HEADS = 8
HEAD_SIZE = 128
BLOCK = 128
FAR = -1e30


def shifted(value, axis, steps):
    count = lax.axis_size(axis)
    return lax.ppermute(value, axis, [(source, (source + steps) % count) for source in range(count)])


def swapped(value, axis, bits):
    count = lax.axis_size(axis)
    return lax.ppermute(value, axis, [(source, source ^ bits) for source in range(count)])


def attention_kernel(chunks, sources_ref, pattern_ref, q_ref, *refs):
    kv_refs, out_ref = refs[:-1], refs[-1]
    tok_dev, width = q_ref.shape
    heads = width // HEAD_SIZE
    blocks_dev = tok_dev // BLOCK
    group = min(heads, 4)
    exponent_scale = math.log2(math.e) / math.sqrt(HEAD_SIZE)
    keys = jnp.concatenate([ref[:, :HEAD_SIZE] for ref in kv_refs], axis=0)
    values = jnp.concatenate([ref[:, HEAD_SIZE:] for ref in kv_refs], axis=0)
    values = jnp.concatenate([values, jnp.ones_like(values)], axis=1)
    own = sources_ref[chunks]
    for a in range(blocks_dev):
        query_block = own * blocks_dev + a
        pieces = []
        for s in range(chunks):
            for j in range(blocks_dev):
                key_block = sources_ref[s] * blocks_dev + j
                on = (pattern_ref[query_block, key_block] == 1) | (query_block == key_block)
                pieces.append(jnp.full((1, BLOCK), jnp.where(on, 0.0, FAR), jnp.float32))
        bias = jnp.concatenate(pieces, axis=1)
        rows = slice(a * BLOCK, (a + 1) * BLOCK)
        for first in range(0, heads, group):
            ids = range(first, first + group)
            q = jnp.concatenate(
                [q_ref[rows, h * HEAD_SIZE : (h + 1) * HEAD_SIZE] for h in ids], axis=0
            )
            scores = lax.dot_general(
                q, keys, (((1,), (1,)), ((), ())), preferred_element_type=jnp.float32
            )
            scores = scores + bias
            top = jnp.max(scores, axis=1, keepdims=True)
            weights = jnp.exp2((scores - top) * exponent_scale).astype(jnp.bfloat16)
            summed = jnp.dot(weights, values, preferred_element_type=jnp.float32)
            result = (summed[:, :HEAD_SIZE] / summed[:, HEAD_SIZE:]).astype(jnp.bfloat16)
            for i, h in enumerate(ids):
                out_ref[rows, h * HEAD_SIZE : (h + 1) * HEAD_SIZE] = result[
                    i * BLOCK : (i + 1) * BLOCK
                ]


def attend(queries, kv_parts, sources, block_pattern):
    chunks = len(kv_parts)
    smem = pl.BlockSpec(memory_space=pltpu.SMEM)
    vmem = pl.BlockSpec(memory_space=pltpu.VMEM)
    return pl.pallas_call(
        functools.partial(attention_kernel, chunks),
        out_shape=jax.ShapeDtypeStruct(queries.shape, jnp.bfloat16),
        in_specs=[smem, smem, vmem] + [vmem] * chunks,
        out_specs=vmem,
        compiler_params=pltpu.CompilerParams(vmem_limit_bytes=40 << 20),
    )(sources, block_pattern, queries, *kv_parts)


def gathered_over_ctx(kv):
    count = lax.axis_size("ctx")
    me = lax.axis_index("ctx")
    if count == 4:
        parts = [kv, shifted(kv, "ctx", 2), shifted(kv, "ctx", 1), shifted(kv, "ctx", 3)]
        steps = jnp.array([0, 2, 1, 3, 0], jnp.int32)
        return parts, (me - steps + count) % count
    whole = lax.all_gather(kv, "ctx")
    sources = jnp.concatenate([jnp.arange(count, dtype=jnp.int32), me[None].astype(jnp.int32)])
    return [whole[i] for i in range(count)], sources


def weight_rows(out_weight, device, rows, first=0):
    return lax.dynamic_slice_in_dim(out_weight, device * rows + first, rows if not first else first, 0)


def on_device(queries, key_vectors, value_head_vectors, block_pattern, out_weight):
    heads_dev = queries.shape[1] // HEAD_SIZE
    query_group_count = QUERY_HEADS // KEY_VALUE_HEADS
    head_count = lax.axis_size("head")
    me = lax.axis_index("head")
    key_head = me * heads_dev // query_group_count
    start = key_head * HEAD_SIZE
    kv = jnp.concatenate(
        [
            lax.dynamic_slice_in_dim(key_vectors, start, HEAD_SIZE, 1),
            lax.dynamic_slice_in_dim(value_head_vectors, start, HEAD_SIZE, 1),
        ],
        axis=1,
    )
    kv_parts, sources = gathered_over_ctx(kv)
    att = attend(queries, kv_parts, sources, block_pattern)

    width = att.shape[1]

    def times(part, owner, first=0):
        rows = lax.dynamic_slice_in_dim(out_weight, owner * width + first, part.shape[1], 0)
        return jnp.dot(part, rows, preferred_element_type=jnp.float32)

    if head_count == 8:
        half = width // 2
        x = swapped(att, "head", 2)
        y = swapped(att, "head", 4)
        sib = swapped(att, "head", 1)
        mixed = times(att, me) + times(sib, me ^ 1)
        xs = swapped(x, "head", 1)
        da = swapped(x[:, :half], "head", 4)
        mixed = mixed + times(x, me ^ 2) + times(xs, me ^ 3)
        ys = swapped(y, "head", 1)
        db = swapped(y[:, half:], "head", 2)
        mixed = mixed + times(y, me ^ 4) + times(ys, me ^ 5)
        das = swapped(da, "head", 1)
        mixed = mixed + times(da, me ^ 6) + times(das, me ^ 7)
        dbs = swapped(db, "head", 1)
        mixed = mixed + times(db, me ^ 6, half) + times(dbs, me ^ 7, half)
    else:
        mixed = jnp.dot(
            lax.all_gather(att, "head", axis=1, tiled=True),
            out_weight,
            preferred_element_type=jnp.float32,
        )
    return mixed.astype(jnp.bfloat16)


def solution(mesh):
    return jax.shard_map(
        on_device,
        mesh=mesh,
        in_specs=(P("ctx", "head"), P("ctx", None), P("ctx", None), P(), P(None, "head")),
        out_specs=P("ctx", "head"),
        check_vma=False,
    )
```

```python
import functools
import math

import jax
import jax.numpy as jnp
from jax import lax
from jax.experimental import pallas as pl
from jax.experimental.pallas import tpu as pltpu
from jax.sharding import PartitionSpec as P

QUERY_HEADS = 64
KEY_VALUE_HEADS = 8
HEAD_SIZE = 128
BLOCK = 128
FAR = -1e30

SMEM = pl.BlockSpec(memory_space=pltpu.SMEM)
VMEM = pl.BlockSpec(memory_space=pltpu.VMEM)
HBM = pl.BlockSpec(memory_space=pltpu.HBM)


def params(mib):
    return pltpu.CompilerParams(vmem_limit_bytes=mib << 20)


def cost(flops, moved):
    return pl.CostEstimate(flops=flops, bytes_accessed=moved, transcendentals=0)


def shifted(value, axis, steps):
    count = lax.axis_size(axis)
    return lax.ppermute(value, axis, [(source, (source + steps) % count) for source in range(count)])


def swapped(value, axis, bits):
    count = lax.axis_size(axis)
    return lax.ppermute(value, axis, [(source, source ^ bits) for source in range(count)])


def staging(places, depth, table_ref, staged_ref, sems):
    me = lax.axis_index("head")
    copies = []
    for slot, (bits, half) in enumerate(places):
        row = pl.multiple_of((me ^ bits) * (2 * depth) + half * depth, depth)
        copies.append(
            pltpu.make_async_copy(
                table_ref.at[pl.ds(row, depth)],
                staged_ref.at[pl.ds(slot * depth, depth)],
                sems.at[slot],
            )
        )
    for copy in copies:
        copy.start()
    return copies


def weights_kernel(steps, count, upcoming, depth, pattern_ref, q_ref, *refs):
    copies = []
    if upcoming:
        *key_refs, table_ref, out_ref, staged_ref, sems = refs
        copies = staging(upcoming, depth, table_ref, staged_ref, sems)
    else:
        *key_refs, out_ref = refs
    tok_dev, width = q_ref.shape
    heads = width // HEAD_SIZE
    blocks_dev = tok_dev // BLOCK
    group = min(heads, 4)
    exponent_scale = math.log2(math.e) / math.sqrt(HEAD_SIZE)
    keys = jnp.concatenate([ref[...] for ref in key_refs], axis=0)
    me = lax.axis_index("ctx")
    for a in range(blocks_dev):
        query_block = me * blocks_dev + a
        pieces = []
        for step in steps:
            source = step if count is None else lax.rem(me + (count - step), count)
            for j in range(blocks_dev):
                key_block = source * blocks_dev + j
                on = (pattern_ref[query_block, key_block] == 1) | (query_block == key_block)
                pieces.append(jnp.full((1, BLOCK), jnp.where(on, 0.0, FAR), jnp.float32))
        bias = jnp.concatenate(pieces, axis=1)
        rows = slice(a * BLOCK, (a + 1) * BLOCK)
        for first in range(0, heads, group):
            q = jnp.concatenate(
                [
                    q_ref[rows, h * HEAD_SIZE : (h + 1) * HEAD_SIZE]
                    for h in range(first, first + group)
                ],
                axis=0,
            )
            scores = lax.dot_general(
                q, keys, (((1,), (1,)), ((), ())), preferred_element_type=jnp.float32
            )
            scores = scores + bias
            top = jnp.max(scores, axis=1, keepdims=True)
            out_ref[a, first * BLOCK : (first + group) * BLOCK, :] = jnp.exp2(
                (scores - top) * exponent_scale
            ).astype(jnp.bfloat16)
    for copy in copies:
        copy.wait()


def weights_of(queries, key_parts, steps, count, block_pattern, table=None, upcoming=()):
    tok_dev, width = queries.shape
    blocks_dev, heads = tok_dev // BLOCK, width // HEAD_SIZE
    keys = sum(part.shape[0] for part in key_parts)
    out_shape = [jax.ShapeDtypeStruct((blocks_dev, heads * BLOCK, keys), jnp.bfloat16)]
    more, scratch = [], []
    depth = width // 2
    if upcoming:
        out_shape.append(
            jax.ShapeDtypeStruct((depth * len(upcoming), table.shape[1]), table.dtype)
        )
        more = [table]
        scratch = [pltpu.SemaphoreType.DMA((len(upcoming),))]
    return pl.pallas_call(
        functools.partial(weights_kernel, steps, count, upcoming, depth),
        out_shape=out_shape,
        in_specs=[SMEM, VMEM] + [VMEM] * len(key_parts) + [HBM] * len(more),
        out_specs=[VMEM] * len(out_shape),
        scratch_shapes=scratch,
        compiler_params=params(32),
        cost_estimate=cost(8 * tok_dev * heads * keys * HEAD_SIZE, 4 << 20),
    )(block_pattern, queries, *key_parts, *more)


def values_kernel(first, group, weights_ref, *refs):
    value_refs, out_ref = refs[:-1], refs[-1]
    values = jnp.concatenate([ref[...] for ref in value_refs], axis=0)
    values = jnp.concatenate([values, jnp.ones_like(values)], axis=1)
    for a in range(weights_ref.shape[0]):
        summed = jnp.dot(
            weights_ref[a, first * BLOCK : (first + group) * BLOCK, :],
            values,
            preferred_element_type=jnp.float32,
        )
        result = (summed[:, :HEAD_SIZE] / summed[:, HEAD_SIZE:]).astype(jnp.bfloat16)
        for i in range(group):
            out_ref[a * BLOCK : (a + 1) * BLOCK, i * HEAD_SIZE : (i + 1) * HEAD_SIZE] = result[
                i * BLOCK : (i + 1) * BLOCK
            ]


def attended_of(weights, value_parts, first, group):
    blocks_dev, _, keys = weights.shape
    return pl.pallas_call(
        functools.partial(values_kernel, first, group),
        out_shape=jax.ShapeDtypeStruct((blocks_dev * BLOCK, group * HEAD_SIZE), jnp.bfloat16),
        in_specs=[VMEM] * (1 + len(value_parts)),
        out_specs=VMEM,
        compiler_params=params(20),
        cost_estimate=cost(4 * blocks_dev * BLOCK * group * keys * HEAD_SIZE, 1 << 20),
    )(weights, *value_parts)


def projection_kernel(count, fresh, upcoming, weight_ref, *refs):
    refs = list(refs)
    total = None if fresh else refs.pop(0)[...]
    parts = refs[:count]
    depth = parts[0].shape[1]
    copies = []
    if upcoming:
        table_ref, out_ref, staged_ref, sems = refs[count:]
        copies = staging(upcoming, depth, table_ref, staged_ref, sems)
    else:
        (out_ref,) = refs[count:]
    for slot, part in enumerate(parts):
        term = jnp.dot(
            part[...],
            weight_ref[slot * depth : (slot + 1) * depth, :],
            preferred_element_type=jnp.float32,
        )
        total = term if total is None else total + term
    out_ref[...] = total.astype(out_ref.dtype)
    for copy in copies:
        copy.wait()


def projected(total, weight, parts, table=None, upcoming=()):
    rows, depth = parts[0].shape
    columns = weight.shape[1]
    fresh = total is None
    operands = [weight] + ([] if fresh else [total]) + parts
    out_shape = [jax.ShapeDtypeStruct((rows, columns), jnp.float32 if upcoming else jnp.bfloat16)]
    more, scratch = [], []
    if upcoming:
        out_shape.append(jax.ShapeDtypeStruct((depth * len(upcoming), columns), weight.dtype))
        more = [table]
        scratch = [pltpu.SemaphoreType.DMA((len(upcoming),))]
    return pl.pallas_call(
        functools.partial(projection_kernel, len(parts), fresh, upcoming),
        out_shape=out_shape,
        in_specs=[VMEM] * len(operands) + [HBM] * len(more),
        out_specs=[VMEM] * len(out_shape),
        scratch_shapes=scratch,
        compiler_params=params(24),
        cost_estimate=cost(16 * rows * depth * columns * len(parts), 1 << 20),
    )(*operands, *more)


def gathered_over_ctx(part):
    if lax.axis_size("ctx") == 4:
        return [part] + [shifted(part, "ctx", step) for step in (2, 1, 3)], (0, 2, 1, 3), 4
    whole = lax.all_gather(part, "ctx")
    count = whole.shape[0]
    return [whole[i] for i in range(count)], tuple(range(count)), None


def on_device(queries, key_vectors, value_head_vectors, block_pattern, out_weight):
    heads_dev = queries.shape[1] // HEAD_SIZE
    query_group_count = QUERY_HEADS // KEY_VALUE_HEADS
    head_count = lax.axis_size("head")
    me = lax.axis_index("head")
    start = (me * heads_dev // query_group_count) * HEAD_SIZE
    keys = lax.dynamic_slice_in_dim(key_vectors, start, HEAD_SIZE, 1)
    values = lax.dynamic_slice_in_dim(value_head_vectors, start, HEAD_SIZE, 1)
    key_parts, steps, count = gathered_over_ctx(keys)
    value_parts, _, _ = gathered_over_ctx(values)
    if head_count != 8:
        (weights,) = weights_of(queries, key_parts, steps, count, block_pattern)
        att = attended_of(weights, value_parts, 0, heads_dev)
        mixed = jnp.dot(
            lax.all_gather(att, "head", axis=1, tiled=True),
            out_weight,
            preferred_element_type=jnp.float32,
        )
        return mixed.astype(jnp.bfloat16)

    own = ((0, 0), (0, 1), (1, 0), (1, 1))
    early = ((2, 0), (3, 0), (4, 1), (5, 1))
    late = ((2, 1), (3, 1), (4, 0), (5, 0))
    across = ((6, 0), (7, 0), (6, 1), (7, 1))
    weights, rows = weights_of(
        queries, key_parts, steps, count, block_pattern, out_weight, own
    )
    half = heads_dev // 2
    a = attended_of(weights, value_parts, 0, half)
    b = attended_of(weights, value_parts, half, half)
    xa = swapped(a, "head", 2)
    yb = swapped(b, "head", 4)
    xb = swapped(b, "head", 2)
    ya = swapped(a, "head", 4)
    sa = swapped(a, "head", 1)
    sb = swapped(b, "head", 1)
    mixed, rows = projected(None, rows, [a, b, sa, sb], out_weight, early)
    da = swapped(xa, "head", 4)
    db = swapped(yb, "head", 2)
    xas, xbs, yas, ybs = [swapped(part, "head", 1) for part in (xa, xb, ya, yb)]
    mixed, rows = projected(mixed, rows, [xa, xas, yb, ybs], out_weight, late)
    mixed, rows = projected(mixed, rows, [xb, xbs, ya, yas], out_weight, across)
    das = swapped(da, "head", 1)
    dbs = swapped(db, "head", 1)
    (mixed,) = projected(mixed, rows, [da, das, db, dbs])
    return mixed


def solution(mesh):
    return jax.shard_map(
        on_device,
        mesh=mesh,
        in_specs=(P("ctx", "head"), P("ctx", None), P("ctx", None), P(), P(None, "head")),
        out_specs=P("ctx", "head"),
        check_vma=False,
    )
```

```python
import functools
import math

import jax
import jax.numpy as jnp
from jax import lax
from jax.experimental import pallas as pl
from jax.experimental.pallas import tpu as pltpu
from jax.sharding import PartitionSpec as P

QUERY_HEADS = 64
KEY_VALUE_HEADS = 8
HEAD_SIZE = 128
BLOCK = 128
FAR = -1e30

SMEM = pl.BlockSpec(memory_space=pltpu.SMEM)
VMEM = pl.BlockSpec(memory_space=pltpu.VMEM)
HBM = pl.BlockSpec(memory_space=pltpu.HBM)


def params(mib):
    return pltpu.CompilerParams(vmem_limit_bytes=mib << 20)


def cost(flops, moved):
    return pl.CostEstimate(flops=flops, bytes_accessed=moved, transcendentals=0)


def shifted(value, axis, steps):
    count = lax.axis_size(axis)
    return lax.ppermute(value, axis, [(source, (source + steps) % count) for source in range(count)])


def swapped(value, axis, bits):
    count = lax.axis_size(axis)
    return lax.ppermute(value, axis, [(source, source ^ bits) for source in range(count)])


def staging(places, depth, table_ref, staged_ref, sems):
    me = lax.axis_index("head")
    copies = []
    for slot, (bits, half) in enumerate(places):
        row = pl.multiple_of((me ^ bits) * (2 * depth) + half * depth, depth)
        copies.append(
            pltpu.make_async_copy(
                table_ref.at[pl.ds(row, depth)],
                staged_ref.at[pl.ds(slot * depth, depth)],
                sems.at[slot],
            )
        )
    for copy in copies:
        copy.start()
    return copies


def own_slices(key_vectors, value_vectors, width):
    heads_dev = width // HEAD_SIZE
    head = lax.axis_index("head") * heads_dev // (QUERY_HEADS // KEY_VALUE_HEADS)
    return lax.optimization_barrier(
        tuple(
            lax.dynamic_slice_in_dim(vectors, head * HEAD_SIZE, HEAD_SIZE, 1)
            for vectors in (key_vectors, value_vectors)
        )
    )


def first_lane(shape):
    return lax.broadcasted_iota(jnp.int32, shape, 1) == 0


def stack_kernel(steps, count, pattern_ref, q_ref, stacked_ref, mask_ref, sems):
    tok_dev, width = q_ref.shape
    heads = width // HEAD_SIZE
    blocks_dev = tok_dev // BLOCK
    copies = []
    for a in range(blocks_dev):
        for h in range(heads):
            copies.append(
                pltpu.make_async_copy(
                    q_ref.at[pl.ds(a * BLOCK, BLOCK), pl.ds(h * HEAD_SIZE, HEAD_SIZE)],
                    stacked_ref.at[a, pl.ds(h * BLOCK, BLOCK)],
                    sems.at[a, h],
                )
            )
    for copy in copies:
        copy.start()
    me = lax.axis_index("ctx")
    lane = first_lane((BLOCK, BLOCK))
    for a in range(blocks_dev):
        query_block = me * blocks_dev + a
        row = 0
        for step in steps:
            source = step if count is None else lax.rem(me + (count - step), count)
            for j in range(blocks_dev):
                key_block = source * blocks_dev + j
                on = (pattern_ref[query_block, key_block] == 1) | (query_block == key_block)
                mask_ref[a, row : row + BLOCK, :] = jnp.where(
                    lane, jnp.where(on, 0.0, FAR), 0.0
                ).astype(jnp.bfloat16)
                row += BLOCK
    for copy in copies:
        copy.wait()


def stacked_of(queries, steps, count, block_pattern):
    tok_dev, width = queries.shape
    blocks_dev, heads = tok_dev // BLOCK, width // HEAD_SIZE
    return pl.pallas_call(
        functools.partial(stack_kernel, steps, count),
        out_shape=[
            jax.ShapeDtypeStruct((blocks_dev, heads * BLOCK, HEAD_SIZE), jnp.bfloat16),
            jax.ShapeDtypeStruct((blocks_dev, len(steps) * tok_dev, BLOCK), jnp.bfloat16),
        ],
        in_specs=[SMEM, HBM],
        out_specs=[VMEM, VMEM],
        scratch_shapes=[pltpu.SemaphoreType.DMA((blocks_dev, heads))],
        compiler_params=params(40),
        cost_estimate=cost(0, 1 << 20),
    )(block_pattern, queries)


def weights_kernel(upcoming, depth, q_ref, mask_ref, *refs):
    copies = []
    if upcoming:
        *key_refs, table_ref, out_ref, staged_ref, sems = refs
        copies = staging(upcoming, depth, table_ref, staged_ref, sems)
    else:
        *key_refs, out_ref = refs
    blocks_dev, rows, _ = q_ref.shape
    group = min(rows, 512)
    exponent_scale = math.log2(math.e) / math.sqrt(HEAD_SIZE)
    keys = jnp.concatenate([ref[...] for ref in key_refs], axis=0)
    lane = jnp.where(first_lane((group, BLOCK)), 1.0, 0.0).astype(jnp.bfloat16)
    for a in range(blocks_dev):
        wide_keys = jnp.concatenate([keys, mask_ref[a]], axis=1)
        for first in range(0, rows, group):
            wide = jnp.concatenate([q_ref[a, first : first + group, :], lane], axis=1)
            scores = lax.dot_general(
                wide, wide_keys, (((1,), (1,)), ((), ())), preferred_element_type=jnp.float32
            )
            top = jnp.max(scores, axis=1, keepdims=True)
            out_ref[a, first : first + group, :] = jnp.exp2(
                (scores - top) * exponent_scale
            ).astype(jnp.bfloat16)
    for copy in copies:
        copy.wait()


def weights_of(stacked, mask, key_parts, table=None, upcoming=()):
    blocks_dev, rows, _ = stacked.shape
    keys = mask.shape[1]
    out_shape = [jax.ShapeDtypeStruct((blocks_dev, rows, keys), jnp.bfloat16)]
    more, scratch = [], []
    depth = rows // 2
    if upcoming:
        out_shape.append(
            jax.ShapeDtypeStruct((depth * len(upcoming), table.shape[1]), table.dtype)
        )
        more = [table]
        scratch = [pltpu.SemaphoreType.DMA((len(upcoming),))]
    return pl.pallas_call(
        functools.partial(weights_kernel, upcoming, depth),
        out_shape=out_shape,
        in_specs=[VMEM] * (2 + len(key_parts)) + [HBM] * len(more),
        out_specs=[VMEM] * len(out_shape),
        scratch_shapes=scratch,
        compiler_params=params(40),
        cost_estimate=cost(8 * blocks_dev * rows * keys * HEAD_SIZE, 4 << 20),
    )(stacked, mask, *key_parts, *more)


def values_kernel(first, group, weights_ref, *refs):
    value_refs, out_ref = refs[:-1], refs[-1]
    values = jnp.concatenate([ref[...] for ref in value_refs], axis=0)
    values = jnp.concatenate([values, jnp.ones_like(values)], axis=1)
    for a in range(weights_ref.shape[0]):
        summed = jnp.dot(
            weights_ref[a, first * BLOCK : (first + group) * BLOCK, :],
            values,
            preferred_element_type=jnp.float32,
        )
        result = (summed[:, :HEAD_SIZE] / summed[:, HEAD_SIZE:]).astype(jnp.bfloat16)
        for i in range(group):
            out_ref[a * BLOCK : (a + 1) * BLOCK, i * HEAD_SIZE : (i + 1) * HEAD_SIZE] = result[
                i * BLOCK : (i + 1) * BLOCK
            ]


def attended_of(weights, value_parts, first, group):
    blocks_dev, _, keys = weights.shape
    return pl.pallas_call(
        functools.partial(values_kernel, first, group),
        out_shape=jax.ShapeDtypeStruct((blocks_dev * BLOCK, group * HEAD_SIZE), jnp.bfloat16),
        in_specs=[VMEM] * (1 + len(value_parts)),
        out_specs=VMEM,
        compiler_params=params(40),
        cost_estimate=cost(4 * blocks_dev * BLOCK * group * keys * HEAD_SIZE, 1 << 20),
    )(weights, *value_parts)


def projection_kernel(count, fresh, upcoming, weight_ref, *refs):
    refs = list(refs)
    total = None if fresh else refs.pop(0)[...]
    parts = refs[:count]
    depth = parts[0].shape[1]
    copies = []
    if upcoming:
        table_ref, out_ref, staged_ref, sems = refs[count:]
        copies = staging(upcoming, depth, table_ref, staged_ref, sems)
    else:
        (out_ref,) = refs[count:]
    term = jnp.dot(
        jnp.concatenate([part[...] for part in parts], axis=1),
        weight_ref[...],
        preferred_element_type=jnp.float32,
    )
    total = term if total is None else total + term
    out_ref[...] = total.astype(out_ref.dtype)
    for copy in copies:
        copy.wait()


def projected(total, weight, parts, table=None, upcoming=()):
    rows, depth = parts[0].shape
    columns = weight.shape[1]
    fresh = total is None
    operands = [weight] + ([] if fresh else [total]) + parts
    out_shape = [jax.ShapeDtypeStruct((rows, columns), jnp.float32 if upcoming else jnp.bfloat16)]
    more, scratch = [], []
    if upcoming:
        out_shape.append(jax.ShapeDtypeStruct((depth * len(upcoming), columns), weight.dtype))
        more = [table]
        scratch = [pltpu.SemaphoreType.DMA((len(upcoming),))]
    return pl.pallas_call(
        functools.partial(projection_kernel, len(parts), fresh, upcoming),
        out_shape=out_shape,
        in_specs=[VMEM] * len(operands) + [HBM] * len(more),
        out_specs=[VMEM] * len(out_shape),
        scratch_shapes=scratch,
        compiler_params=params(40),
        cost_estimate=cost(16 * rows * depth * columns * len(parts), 1 << 20),
    )(*operands, *more)


def gathered_over_ctx(part):
    if lax.axis_size("ctx") == 4:
        return [part] + [shifted(part, "ctx", step) for step in (2, 1, 3)], (0, 2, 1, 3), 4
    whole = lax.all_gather(part, "ctx")
    count = whole.shape[0]
    return [whole[i] for i in range(count)], tuple(range(count)), None


def on_device(queries, key_vectors, value_head_vectors, block_pattern, out_weight):
    heads_dev = queries.shape[1] // HEAD_SIZE
    keys, values = own_slices(key_vectors, value_head_vectors, queries.shape[1])
    key_parts, steps, count = gathered_over_ctx(keys)
    value_parts, _, _ = gathered_over_ctx(values)
    stacked, mask = stacked_of(queries, steps, count, block_pattern)
    if lax.axis_size("head") != 8:
        (weights,) = weights_of(stacked, mask, key_parts)
        att = attended_of(weights, value_parts, 0, heads_dev)
        mixed = jnp.dot(
            lax.all_gather(att, "head", axis=1, tiled=True),
            out_weight,
            preferred_element_type=jnp.float32,
        )
        return mixed.astype(jnp.bfloat16)

    own = ((0, 0), (0, 1), (1, 0), (1, 1))
    early = ((2, 0), (3, 0), (4, 1), (5, 1))
    late = ((2, 1), (3, 1), (4, 0), (5, 0))
    across = ((6, 0), (7, 0), (6, 1), (7, 1))
    weights, rows = weights_of(stacked, mask, key_parts, out_weight, own)
    half = heads_dev // 2
    a = attended_of(weights, value_parts, 0, half)
    b = attended_of(weights, value_parts, half, half)
    xa = swapped(a, "head", 2)
    yb = swapped(b, "head", 4)
    xb = swapped(b, "head", 2)
    ya = swapped(a, "head", 4)
    sa = swapped(a, "head", 1)
    sb = swapped(b, "head", 1)
    mixed, rows = projected(None, rows, [a, b, sa, sb], out_weight, early)
    xa, mixed = lax.optimization_barrier((xa, mixed))
    da = swapped(xa, "head", 4)
    yb, mixed = lax.optimization_barrier((yb, mixed))
    db = swapped(yb, "head", 2)
    xas, xbs, yas, ybs = [swapped(part, "head", 1) for part in (xa, xb, ya, yb)]
    mixed, rows = projected(mixed, rows, [xa, xas, yb, ybs], out_weight, late)
    mixed, rows = projected(mixed, rows, [xb, xbs, ya, yas], out_weight, across)
    das = swapped(da, "head", 1)
    dbs = swapped(db, "head", 1)
    (mixed,) = projected(mixed, rows, [da, das, db, dbs])
    return mixed


def solution(mesh):
    return jax.shard_map(
        on_device,
        mesh=mesh,
        in_specs=(P("ctx", "head"), P("ctx", None), P("ctx", None), P(), P(None, "head")),
        out_specs=P("ctx", "head"),
        check_vma=False,
    )
```

```python
import functools
import math

import jax
import jax.numpy as jnp
from jax import lax
from jax.experimental import pallas as pl
from jax.experimental.pallas import tpu as pltpu
from jax.sharding import PartitionSpec as P

QUERY_HEADS = 64
KEY_VALUE_HEADS = 8
HEAD_SIZE = 128
BLOCK = 128
FAR = -1e30

SMEM = pl.BlockSpec(memory_space=pltpu.SMEM)
VMEM = pl.BlockSpec(memory_space=pltpu.VMEM)
HBM = pl.BlockSpec(memory_space=pltpu.HBM)


def params(mib):
    return pltpu.CompilerParams(vmem_limit_bytes=mib << 20)


def held(shape, dtype=jnp.bfloat16):
    return pltpu.VMEM(shape, dtype)


def cost(flops, moved):
    return pl.CostEstimate(flops=flops, bytes_accessed=moved, transcendentals=0)


def shifted(value, axis, steps):
    count = lax.axis_size(axis)
    return lax.ppermute(value, axis, [(source, (source + steps) % count) for source in range(count)])


def swapped(value, axis, bits):
    count = lax.axis_size(axis)
    return lax.ppermute(value, axis, [(source, source ^ bits) for source in range(count)])


def first_lane(shape):
    return lax.broadcasted_iota(jnp.int32, shape, 1) == 0


def prepare_kernel(steps, count, keys_ref, values_ref, q_ref, pattern_ref, *refs):
    own_keys_ref, own_values_ref, stacked_ref, mask_ref, table_ref, sems, stack_sems = refs
    tok_dev, width = q_ref.shape
    heads = width // HEAD_SIZE
    blocks_dev = tok_dev // BLOCK
    head = lax.div(lax.axis_index("head") * heads, QUERY_HEADS // KEY_VALUE_HEADS)
    columns = pl.ds(pl.multiple_of(head * HEAD_SIZE, HEAD_SIZE), HEAD_SIZE)
    table = pltpu.make_async_copy(pattern_ref, table_ref, sems.at[2])
    copies = [
        pltpu.make_async_copy(keys_ref.at[:, columns], own_keys_ref, sems.at[0]),
        pltpu.make_async_copy(values_ref.at[:, columns], own_values_ref, sems.at[1]),
    ]
    for a in range(blocks_dev):
        for h in range(heads):
            copies.append(
                pltpu.make_async_copy(
                    q_ref.at[pl.ds(a * BLOCK, BLOCK), pl.ds(h * HEAD_SIZE, HEAD_SIZE)],
                    stacked_ref.at[a, pl.ds(h * BLOCK, BLOCK)],
                    stack_sems.at[a, h],
                )
            )
    table.start()
    for copy in copies:
        copy.start()
    table.wait()
    me = lax.axis_index("ctx")
    lane = first_lane((BLOCK, BLOCK))
    for a in range(blocks_dev):
        query_block = me * blocks_dev + a
        row = 0
        for step in steps:
            source = step if count is None else lax.rem(me + (count - step), count)
            for j in range(blocks_dev):
                key_block = source * blocks_dev + j
                on = (table_ref[query_block, key_block] == 1) | (query_block == key_block)
                mask_ref[a, row : row + BLOCK, :] = jnp.where(
                    lane, jnp.where(on, 0.0, FAR), 0.0
                ).astype(jnp.bfloat16)
                row += BLOCK
    for copy in copies:
        copy.wait()


def prepared(key_vectors, value_vectors, queries, block_pattern, steps, count):
    tok_dev, width = queries.shape
    blocks_dev, heads = tok_dev // BLOCK, width // HEAD_SIZE
    own = held((tok_dev, HEAD_SIZE))
    return pl.pallas_call(
        functools.partial(prepare_kernel, steps, count),
        out_shape=[
            own,
            own,
            held((blocks_dev, heads * BLOCK, HEAD_SIZE)),
            held((blocks_dev, len(steps) * tok_dev, BLOCK)),
        ],
        in_specs=[HBM] * 4,
        out_specs=[VMEM] * 4,
        scratch_shapes=[
            pltpu.SMEM(block_pattern.shape, jnp.int32),
            pltpu.SemaphoreType.DMA((3,)),
            pltpu.SemaphoreType.DMA((blocks_dev, heads)),
        ],
        compiler_params=params(8),
        cost_estimate=cost(0, 1 << 20),
    )(
        *[
            pltpu.with_memory_space_constraint(operand, pltpu.HBM)
            for operand in (key_vectors, value_vectors, queries, block_pattern)
        ]
    )


def weights_kernel(q_ref, mask_ref, *refs):
    *key_refs, out_ref = refs
    blocks_dev, rows, _ = q_ref.shape
    group = min(rows, 512)
    exponent_scale = math.log2(math.e) / math.sqrt(HEAD_SIZE)
    keys = jnp.concatenate([ref[...] for ref in key_refs], axis=0)
    lane = jnp.where(first_lane((group, BLOCK)), 1.0, 0.0).astype(jnp.bfloat16)
    for a in range(blocks_dev):
        wide_keys = jnp.concatenate([keys, mask_ref[a]], axis=1)
        for first in range(0, rows, group):
            wide = jnp.concatenate([q_ref[a, first : first + group, :], lane], axis=1)
            scores = lax.dot_general(
                wide, wide_keys, (((1,), (1,)), ((), ())), preferred_element_type=jnp.float32
            )
            top = jnp.max(scores, axis=1, keepdims=True)
            out_ref[a, first : first + group, :] = jnp.exp2(
                (scores - top) * exponent_scale
            ).astype(jnp.bfloat16)


def weights_of(stacked, mask, key_parts):
    blocks_dev, rows, _ = stacked.shape
    keys = mask.shape[1]
    return pl.pallas_call(
        weights_kernel,
        out_shape=held((blocks_dev, rows, keys)),
        in_specs=[VMEM] * (2 + len(key_parts)),
        out_specs=VMEM,
        compiler_params=params(8 + (min(rows, 512) * keys * 16 >> 20)),
        cost_estimate=cost(8 * blocks_dev * rows * keys * HEAD_SIZE, 4 << 20),
    )(stacked, mask, *key_parts)


def values_kernel(first, group, weights_ref, *refs):
    value_refs, out_ref = refs[:-1], refs[-1]
    values = jnp.concatenate([ref[...] for ref in value_refs], axis=0)
    values = jnp.concatenate([values, jnp.ones_like(values)], axis=1)
    for a in range(weights_ref.shape[0]):
        summed = jnp.dot(
            weights_ref[a, first * BLOCK : (first + group) * BLOCK, :],
            values,
            preferred_element_type=jnp.float32,
        )
        result = (summed[:, :HEAD_SIZE] / summed[:, HEAD_SIZE:]).astype(jnp.bfloat16)
        for i in range(group):
            out_ref[a * BLOCK : (a + 1) * BLOCK, i * HEAD_SIZE : (i + 1) * HEAD_SIZE] = result[
                i * BLOCK : (i + 1) * BLOCK
            ]


def attended_of(weights, value_parts, first, group):
    blocks_dev, _, keys = weights.shape
    return pl.pallas_call(
        functools.partial(values_kernel, first, group),
        out_shape=held((blocks_dev * BLOCK, group * HEAD_SIZE)),
        in_specs=[VMEM] * (1 + len(value_parts)),
        out_specs=VMEM,
        compiler_params=params(16),
        cost_estimate=cost(4 * blocks_dev * BLOCK * group * keys * HEAD_SIZE, 1 << 20),
    )(weights, *value_parts)


def projection_kernel(places, fresh, weight_ref, *refs):
    *parts, out_ref = refs
    total = None if fresh else parts.pop(0)[...]
    me = lax.axis_index("head")
    for (bits, half), part in zip(places, parts):
        depth = part.shape[1]
        row = pl.multiple_of((me ^ bits) * (2 * depth) + half * depth, depth)
        term = jnp.dot(
            part[...], weight_ref[pl.ds(row, depth), :], preferred_element_type=jnp.float32
        )
        total = term if total is None else total + term
    out_ref[...] = total.astype(out_ref.dtype)


def projected(total, weight, places, parts, last=False):
    rows, depth = parts[0].shape
    columns = weight.shape[1]
    fresh = total is None
    operands = ([] if fresh else [total]) + parts
    shape = (rows, columns)
    return pl.pallas_call(
        functools.partial(projection_kernel, places, fresh),
        out_shape=jax.ShapeDtypeStruct(shape, jnp.bfloat16) if last else held(shape, jnp.float32),
        in_specs=[VMEM] * (1 + len(operands)),
        out_specs=VMEM,
        compiler_params=params(8),
        cost_estimate=cost(8 * rows * depth * columns * len(parts), 1 << 20),
    )(weight, *operands)


def gathered_over_ctx(part, steps):
    if len(steps) == 4:
        return [part] + [shifted(part, "ctx", step) for step in steps[1:]]
    whole = lax.all_gather(part, "ctx")
    return [whole[i] for i in range(len(steps))]


def on_device(queries, key_vectors, value_head_vectors, block_pattern, out_weight):
    heads_dev = queries.shape[1] // HEAD_SIZE
    count = lax.axis_size("ctx")
    steps = (0, 2, 1, 3) if count == 4 else tuple(range(count))
    keys, values, stacked, mask = prepared(
        key_vectors,
        value_head_vectors,
        queries,
        block_pattern,
        steps,
        count if count == 4 else None,
    )
    key_parts = gathered_over_ctx(keys, steps)
    value_parts = gathered_over_ctx(values, steps)
    weights = weights_of(stacked, mask, key_parts)
    if lax.axis_size("head") != 8:
        att = attended_of(weights, value_parts, 0, heads_dev)
        mixed = jnp.dot(
            lax.all_gather(att, "head", axis=1, tiled=True),
            out_weight,
            preferred_element_type=jnp.float32,
        )
        return mixed.astype(jnp.bfloat16)

    barrier = lax.optimization_barrier
    weight = pltpu.with_memory_space_constraint(out_weight, pltpu.VMEM)
    half = heads_dev // 2
    a = attended_of(weights, value_parts, 0, half)
    b = attended_of(weights, value_parts, half, half)
    xa = swapped(a, "head", 2)
    yb = swapped(b, "head", 4)
    xb = swapped(b, "head", 2)
    ya = swapped(a, "head", 4)
    a, b = barrier((a, b))
    sa = swapped(a, "head", 1)
    sb = swapped(b, "head", 1)
    mixed = projected(None, weight, ((0, 0), (0, 1), (1, 0), (1, 1)), [a, b, sa, sb])
    xa, mixed = barrier((xa, mixed))
    da = swapped(xa, "head", 4)
    yb, mixed = barrier((yb, mixed))
    db = swapped(yb, "head", 2)
    xas, ybs = swapped(xa, "head", 1), swapped(yb, "head", 1)
    mixed = projected(mixed, weight, ((2, 0), (3, 0), (4, 1), (5, 1)), [xa, xas, yb, ybs])

    xbs, yas = swapped(xb, "head", 1), swapped(ya, "head", 1)
    mixed = projected(mixed, weight, ((2, 1), (3, 1), (4, 0), (5, 0)), [xb, xbs, ya, yas])
    da, mixed = barrier((da, mixed))
    das = swapped(da, "head", 1)
    mixed = projected(mixed, weight, ((6, 0), (7, 0)), [da, das])
    dbs = swapped(db, "head", 1)
    return projected(mixed, weight, ((6, 1), (7, 1)), [db, dbs], True)


def solution(mesh):
    return jax.shard_map(
        on_device,
        mesh=mesh,
        in_specs=(P("ctx", "head"), P("ctx", None), P("ctx", None), P(), P(None, "head")),
        out_specs=P("ctx", "head"),
        check_vma=False,
    )
```

```python
import functools
import math

import jax
import jax.numpy as jnp
from jax import lax
from jax.experimental import pallas as pl
from jax.experimental.pallas import tpu as pltpu
from jax.sharding import PartitionSpec as P

QUERY_HEADS = 64
KEY_VALUE_HEADS = 8
HEAD_SIZE = 128
BLOCK = 128
FAR = -1e30

SMEM = pl.BlockSpec(memory_space=pltpu.SMEM)
VMEM = pl.BlockSpec(memory_space=pltpu.VMEM)
HBM = pl.BlockSpec(memory_space=pltpu.HBM)


def params(mib):
    return pltpu.CompilerParams(vmem_limit_bytes=mib << 20)


def held(shape, dtype=jnp.bfloat16):
    return pltpu.VMEM(shape, dtype)


def in_hbm(value):
    return pltpu.with_memory_space_constraint(value, pltpu.HBM)


def cost(flops, moved):
    return pl.CostEstimate(flops=flops, bytes_accessed=moved, transcendentals=0)


def shifted(value, axis, steps):
    count = lax.axis_size(axis)
    return lax.ppermute(value, axis, [(source, (source + steps) % count) for source in range(count)])


def swapped(value, axis, bits):
    count = lax.axis_size(axis)
    return lax.ppermute(value, axis, [(source, source ^ bits) for source in range(count)])


def first_lane(shape):
    return lax.broadcasted_iota(jnp.int32, shape, 1) == 0


def slice_kernel(width, keys_ref, values_ref, own_keys_ref, own_values_ref, sems):
    heads = width // HEAD_SIZE
    head = lax.div(lax.axis_index("head") * heads, QUERY_HEADS // KEY_VALUE_HEADS)
    columns = pl.ds(pl.multiple_of(head * HEAD_SIZE, HEAD_SIZE), HEAD_SIZE)
    copies = [
        pltpu.make_async_copy(keys_ref.at[:, columns], own_keys_ref, sems.at[0]),
        pltpu.make_async_copy(values_ref.at[:, columns], own_values_ref, sems.at[1]),
    ]
    for copy in copies:
        copy.start()
    for copy in copies:
        copy.wait()


def own_slices(key_vectors, value_vectors, width):
    own = held((key_vectors.shape[0], HEAD_SIZE))
    return pl.pallas_call(
        functools.partial(slice_kernel, width),
        out_shape=[own, own],
        in_specs=[HBM] * 2,
        out_specs=[VMEM] * 2,
        scratch_shapes=[pltpu.SemaphoreType.DMA((2,))],
        compiler_params=params(8),
        cost_estimate=cost(0, 1 << 18),
    )(in_hbm(key_vectors), in_hbm(value_vectors))


def stack_kernel(steps, count, q_ref, pattern_ref, *refs):
    stacked_ref, mask_ref, table_ref, table_sem, sems = refs
    blocks_dev, rows, _ = stacked_ref.shape
    heads = rows // BLOCK
    table = pltpu.make_async_copy(pattern_ref, table_ref, table_sem)
    table.start()
    copies = []
    for a in range(blocks_dev):
        for h in range(heads):
            copies.append(
                pltpu.make_async_copy(
                    q_ref.at[pl.ds(a * BLOCK, BLOCK), pl.ds(h * HEAD_SIZE, HEAD_SIZE)],
                    stacked_ref.at[a, pl.ds(h * BLOCK, BLOCK)],
                    sems.at[a, h],
                )
            )
    for copy in copies:
        copy.start()
    table.wait()
    me = lax.axis_index("ctx")
    lane = first_lane((BLOCK, BLOCK))
    for a in range(blocks_dev):
        query_block = me * blocks_dev + a
        row = 0
        for step in steps:
            source = step if count is None else lax.rem(me + (count - step), count)
            for j in range(blocks_dev):
                key_block = source * blocks_dev + j
                on = (table_ref[query_block, key_block] == 1) | (query_block == key_block)
                mask_ref[a, row : row + BLOCK, :] = jnp.where(
                    lane, jnp.where(on, 0.0, FAR), 0.0
                ).astype(jnp.bfloat16)
                row += BLOCK
    for copy in copies:
        copy.wait()


def stacked_of(queries, block_pattern, steps, count):
    tok_dev, width = queries.shape
    blocks_dev, heads = tok_dev // BLOCK, width // HEAD_SIZE
    return pl.pallas_call(
        functools.partial(stack_kernel, steps, count),
        out_shape=[
            held((blocks_dev, heads * BLOCK, HEAD_SIZE)),
            held((blocks_dev, len(steps) * tok_dev, BLOCK)),
        ],
        in_specs=[HBM] * 2,
        out_specs=[VMEM] * 2,
        scratch_shapes=[
            pltpu.SMEM(block_pattern.shape, jnp.int32),
            pltpu.SemaphoreType.DMA(()),
            pltpu.SemaphoreType.DMA((blocks_dev, heads)),
        ],
        compiler_params=params(8),
        cost_estimate=cost(0, 1 << 20),
    )(in_hbm(queries), in_hbm(block_pattern))


def weights_kernel(q_ref, mask_ref, *refs):
    *key_refs, out_ref = refs
    blocks_dev, rows, _ = q_ref.shape
    group = min(rows, 512)
    exponent_scale = math.log2(math.e) / math.sqrt(HEAD_SIZE)
    keys = jnp.concatenate([ref[...] for ref in key_refs], axis=0)
    lane = jnp.where(first_lane((group, BLOCK)), 1.0, 0.0).astype(jnp.bfloat16)
    for a in range(blocks_dev):
        wide_keys = jnp.concatenate([keys, mask_ref[a]], axis=1)
        for first in range(0, rows, group):
            wide = jnp.concatenate([q_ref[a, first : first + group, :], lane], axis=1)
            scores = lax.dot_general(
                wide, wide_keys, (((1,), (1,)), ((), ())), preferred_element_type=jnp.float32
            )
            top = jnp.max(scores, axis=1, keepdims=True)
            out_ref[a, first : first + group, :] = jnp.exp2(
                (scores - top) * exponent_scale
            ).astype(jnp.bfloat16)


def weights_of(stacked, mask, key_parts):
    blocks_dev, rows, _ = stacked.shape
    keys = mask.shape[1]
    return pl.pallas_call(
        weights_kernel,
        out_shape=held((blocks_dev, rows, keys)),
        in_specs=[VMEM] * (2 + len(key_parts)),
        out_specs=VMEM,
        compiler_params=params(8 + (min(rows, 512) * keys * 16 >> 20)),
        cost_estimate=cost(8 * blocks_dev * rows * keys * HEAD_SIZE, 4 << 20),
    )(stacked, mask, *key_parts)


def values_kernel(first, group, weights_ref, *refs):
    value_refs, out_ref = refs[:-1], refs[-1]
    values = jnp.concatenate([ref[...] for ref in value_refs], axis=0)
    values = jnp.concatenate([values, jnp.ones_like(values)], axis=1)
    for a in range(weights_ref.shape[0]):
        summed = jnp.dot(
            weights_ref[a, first * BLOCK : (first + group) * BLOCK, :],
            values,
            preferred_element_type=jnp.float32,
        )
        result = (summed[:, :HEAD_SIZE] / summed[:, HEAD_SIZE:]).astype(jnp.bfloat16)
        for i in range(group):
            out_ref[a * BLOCK : (a + 1) * BLOCK, i * HEAD_SIZE : (i + 1) * HEAD_SIZE] = result[
                i * BLOCK : (i + 1) * BLOCK
            ]


def attended_of(weights, value_parts, first, group):
    blocks_dev, _, keys = weights.shape
    return pl.pallas_call(
        functools.partial(values_kernel, first, group),
        out_shape=held((blocks_dev * BLOCK, group * HEAD_SIZE)),
        in_specs=[VMEM] * (1 + len(value_parts)),
        out_specs=VMEM,
        compiler_params=params(16),
        cost_estimate=cost(4 * blocks_dev * BLOCK * group * keys * HEAD_SIZE, 1 << 20),
    )(weights, *value_parts)


def projection_kernel(places, width, fresh, last, weight_ref, *refs):
    refs = list(refs)
    total_ref = None if fresh else refs.pop(0)
    parts = refs[: len(places)]
    out_ref = refs[len(places)]
    columns = weight_ref.shape[1]
    tile = columns // 4 if last else columns
    me = lax.axis_index("head")
    copies = []
    for n in range(0, columns, tile):
        total = None if fresh else total_ref[:, n : n + tile]
        for (bits, offset), part in zip(places, parts):
            depth = part.shape[1]
            row = pl.multiple_of((me ^ bits) * width + offset, depth)
            term = jnp.dot(
                part[...],
                weight_ref[pl.ds(row, depth), n : n + tile],
                preferred_element_type=jnp.float32,
            )
            total = term if total is None else total + term
        if last:
            held_ref, sems = refs[len(places) + 1 :]
            held_ref[:, n : n + tile] = total.astype(held_ref.dtype)
            copy = pltpu.make_async_copy(
                held_ref.at[:, pl.ds(n, tile)], out_ref.at[:, pl.ds(n, tile)], sems.at[n // tile]
            )
            copy.start()
            copies.append(copy)
        else:
            out_ref[...] = total
    for copy in copies:
        copy.wait()


def projected(total, weight, width, places, parts, last=False):
    rows = parts[0].shape[0]
    columns = weight.shape[1]
    fresh = total is None
    operands = ([] if fresh else [total]) + parts
    shape = (rows, columns)
    depth = sum(part.shape[1] for part in parts)
    return pl.pallas_call(
        functools.partial(projection_kernel, places, width, fresh, last),
        out_shape=jax.ShapeDtypeStruct(shape, jnp.bfloat16) if last else held(shape, jnp.float32),
        in_specs=[VMEM] * (1 + len(operands)),
        out_specs=HBM if last else VMEM,
        scratch_shapes=[pltpu.VMEM(shape, jnp.bfloat16), pltpu.SemaphoreType.DMA((4,))]
        if last
        else [],
        compiler_params=params(8),
        cost_estimate=cost(8 * rows * depth * columns, 1 << 20),
    )(weight, *operands)


def gathered_over_ctx(part, steps):
    if len(steps) == 4:
        return [part] + [shifted(part, "ctx", step) for step in steps[1:]]
    whole = lax.all_gather(part, "ctx")
    return [whole[i] for i in range(len(steps))]


def on_device(queries, key_vectors, value_head_vectors, block_pattern, out_weight):
    heads_dev = queries.shape[1] // HEAD_SIZE
    count = lax.axis_size("ctx")
    steps = (0, 2, 1, 3) if count == 4 else tuple(range(count))
    barrier = lax.optimization_barrier
    keys, values = own_slices(key_vectors, value_head_vectors, queries.shape[1])
    key_parts = gathered_over_ctx(keys, steps)
    value_parts = gathered_over_ctx(values, steps)
    if count == 4:
        key_parts[2], queries = barrier((key_parts[2], queries))
    stacked, mask = stacked_of(queries, block_pattern, steps, count if count == 4 else None)
    weights = weights_of(stacked, mask, key_parts)
    if lax.axis_size("head") != 8:
        att = attended_of(weights, value_parts, 0, heads_dev)
        mixed = jnp.dot(
            lax.all_gather(att, "head", axis=1, tiled=True),
            out_weight,
            preferred_element_type=jnp.float32,
        )
        return mixed.astype(jnp.bfloat16)

    barrier = lax.optimization_barrier
    weight = pltpu.with_memory_space_constraint(out_weight, pltpu.VMEM)
    half = heads_dev // 2
    a = attended_of(weights, value_parts, 0, half)
    b = attended_of(weights, value_parts, half, half)
    xa = swapped(a, "head", 2)
    yb = swapped(b, "head", 4)
    xb = swapped(b, "head", 2)
    ya = swapped(a, "head", 4)
    a, b = barrier((a, b))
    sa = swapped(a, "head", 1)
    sb = swapped(b, "head", 1)
    width, half = heads_dev * HEAD_SIZE, heads_dev * HEAD_SIZE // 2
    mixed = projected(
        None, weight, width, ((0, 0), (0, half), (1, 0), (1, half)), [a, b, sa, sb]
    )
    xa, mixed = barrier((xa, mixed))
    da = swapped(xa, "head", 4)
    yb, mixed = barrier((yb, mixed))
    db = swapped(yb, "head", 2)
    xas, ybs = swapped(xa, "head", 1), swapped(yb, "head", 1)
    mixed = projected(
        mixed, weight, width, ((2, 0), (3, 0), (4, half), (5, half)), [xa, xas, yb, ybs]
    )
    xbs, yas = swapped(xb, "head", 1), swapped(ya, "head", 1)
    mixed = projected(
        mixed, weight, width, ((2, half), (3, half), (4, 0), (5, 0)), [xb, xbs, ya, yas]
    )
    da, mixed = barrier((da, mixed))
    das = swapped(da, "head", 1)
    mixed = projected(mixed, weight, width, ((6, 0), (7, 0)), [da, das])
    dbs = swapped(db, "head", 1)
    return projected(mixed, weight, width, ((6, half), (7, half)), [db, dbs], True)


def solution(mesh):
    return jax.shard_map(
        on_device,
        mesh=mesh,
        in_specs=(P("ctx", "head"), P("ctx", None), P("ctx", None), P(), P(None, "head")),
        out_specs=P("ctx", "head"),
        check_vma=False,
    )
```

```python
import functools
import math

import jax
import jax.numpy as jnp
from jax import lax
from jax.experimental import pallas as pl
from jax.experimental.pallas import tpu as pltpu
from jax.sharding import PartitionSpec as P

QUERY_HEADS = 64
KEY_VALUE_HEADS = 8
HEAD_SIZE = 128
BLOCK = 128
FAR = -1e30

SMEM = pl.BlockSpec(memory_space=pltpu.SMEM)
VMEM = pl.BlockSpec(memory_space=pltpu.VMEM)
HBM = pl.BlockSpec(memory_space=pltpu.HBM)


def params(mib):
    return pltpu.CompilerParams(vmem_limit_bytes=mib << 20)


def held(shape, dtype=jnp.bfloat16):
    return pltpu.VMEM(shape, dtype)


def in_hbm(value):
    return pltpu.with_memory_space_constraint(value, pltpu.HBM)


def cost(flops, moved):
    return pl.CostEstimate(flops=flops, bytes_accessed=moved, transcendentals=0)


def shifted(value, axis, steps):
    count = lax.axis_size(axis)
    return lax.ppermute(value, axis, [(source, (source + steps) % count) for source in range(count)])


def swapped(value, axis, bits):
    count = lax.axis_size(axis)
    return lax.ppermute(value, axis, [(source, source ^ bits) for source in range(count)])


def first_lane(shape):
    return lax.broadcasted_iota(jnp.int32, shape, 1) == 0


def slice_kernel(width, keys_ref, values_ref, own_keys_ref, own_values_ref, sems):
    heads = width // HEAD_SIZE
    head = lax.div(lax.axis_index("head") * heads, QUERY_HEADS // KEY_VALUE_HEADS)
    columns = pl.ds(pl.multiple_of(head * HEAD_SIZE, HEAD_SIZE), HEAD_SIZE)
    copies = [
        pltpu.make_async_copy(keys_ref.at[:, columns], own_keys_ref, sems.at[0]),
        pltpu.make_async_copy(values_ref.at[:, columns], own_values_ref, sems.at[1]),
    ]
    for copy in copies:
        copy.start()
    for copy in copies:
        copy.wait()


def own_slices(key_vectors, value_vectors, width):
    own = held((key_vectors.shape[0], HEAD_SIZE))
    return pl.pallas_call(
        functools.partial(slice_kernel, width),
        out_shape=[own, own],
        in_specs=[HBM] * 2,
        out_specs=[VMEM] * 2,
        scratch_shapes=[pltpu.SemaphoreType.DMA((2,))],
        compiler_params=params(8),
        cost_estimate=cost(0, 1 << 18),
    )(in_hbm(key_vectors), in_hbm(value_vectors))


def stack_kernel(steps, count, q_ref, pattern_ref, *refs):
    stacked_ref, mask_ref, table_ref, table_sem, sems = refs
    blocks_dev, rows, _ = stacked_ref.shape
    heads = rows // BLOCK
    table = pltpu.make_async_copy(pattern_ref, table_ref, table_sem)
    table.start()
    copies = []
    for a in range(blocks_dev):
        for h in range(heads):
            copies.append(
                pltpu.make_async_copy(
                    q_ref.at[pl.ds(a * BLOCK, BLOCK), pl.ds(h * HEAD_SIZE, HEAD_SIZE)],
                    stacked_ref.at[a, pl.ds(h * BLOCK, BLOCK)],
                    sems.at[a, h],
                )
            )
    for copy in copies:
        copy.start()
    table.wait()
    me = lax.axis_index("ctx")
    lane = first_lane((BLOCK, BLOCK))
    for a in range(blocks_dev):
        query_block = me * blocks_dev + a
        row = 0
        for step in steps:
            source = step if count is None else lax.rem(me + (count - step), count)
            for j in range(blocks_dev):
                key_block = source * blocks_dev + j
                on = (table_ref[query_block, key_block] == 1) | (query_block == key_block)
                mask_ref[a, row : row + BLOCK, :] = jnp.where(
                    lane, jnp.where(on, 0.0, FAR), 0.0
                ).astype(jnp.bfloat16)
                row += BLOCK
    for copy in copies:
        copy.wait()


def stacked_of(queries, block_pattern, steps, count):
    tok_dev, width = queries.shape
    blocks_dev, heads = tok_dev // BLOCK, width // HEAD_SIZE
    return pl.pallas_call(
        functools.partial(stack_kernel, steps, count),
        out_shape=[
            held((blocks_dev, heads * BLOCK, HEAD_SIZE)),
            held((blocks_dev, len(steps) * tok_dev, BLOCK)),
        ],
        in_specs=[HBM] * 2,
        out_specs=[VMEM] * 2,
        scratch_shapes=[
            pltpu.SMEM(block_pattern.shape, jnp.int32),
            pltpu.SemaphoreType.DMA(()),
            pltpu.SemaphoreType.DMA((blocks_dev, heads)),
        ],
        compiler_params=params(8),
        cost_estimate=cost(0, 1 << 20),
    )(in_hbm(queries), in_hbm(block_pattern))


def weights_kernel(q_ref, mask_ref, *refs):
    *key_refs, out_ref = refs
    blocks_dev, rows, _ = q_ref.shape
    group = min(rows, 512)
    exponent_scale = math.log2(math.e) / math.sqrt(HEAD_SIZE)
    keys = jnp.concatenate([ref[...] for ref in key_refs], axis=0)
    lane = jnp.where(first_lane((group, BLOCK)), 1.0, 0.0).astype(jnp.bfloat16)
    for a in range(blocks_dev):
        wide_keys = jnp.concatenate([keys, mask_ref[a]], axis=1)
        for first in range(0, rows, group):
            wide = jnp.concatenate([q_ref[a, first : first + group, :], lane], axis=1)
            scores = lax.dot_general(
                wide, wide_keys, (((1,), (1,)), ((), ())), preferred_element_type=jnp.float32
            )
            top = jnp.max(scores, axis=1, keepdims=True)
            out_ref[a, first : first + group, :] = jnp.exp2(
                (scores - top) * exponent_scale
            ).astype(jnp.bfloat16)


def weights_of(stacked, mask, key_parts):
    blocks_dev, rows, _ = stacked.shape
    keys = mask.shape[1]
    return pl.pallas_call(
        weights_kernel,
        out_shape=held((blocks_dev, rows, keys)),
        in_specs=[VMEM] * (2 + len(key_parts)),
        out_specs=VMEM,
        compiler_params=params(8 + (min(rows, 512) * keys * 16 >> 20)),
        cost_estimate=cost(8 * blocks_dev * rows * keys * HEAD_SIZE, 4 << 20),
    )(stacked, mask, *key_parts)


def values_kernel(first, group, weights_ref, *refs):
    value_refs, out_ref = refs[:-1], refs[-1]
    values = jnp.concatenate([ref[...] for ref in value_refs], axis=0)
    values = jnp.concatenate([values, jnp.ones_like(values)], axis=1)
    for a in range(weights_ref.shape[0]):
        summed = jnp.dot(
            weights_ref[a, first * BLOCK : (first + group) * BLOCK, :],
            values,
            preferred_element_type=jnp.float32,
        )
        result = (summed[:, :HEAD_SIZE] / summed[:, HEAD_SIZE:]).astype(jnp.bfloat16)
        for i in range(group):
            out_ref[a * BLOCK : (a + 1) * BLOCK, i * HEAD_SIZE : (i + 1) * HEAD_SIZE] = result[
                i * BLOCK : (i + 1) * BLOCK
            ]


def attended_of(weights, value_parts, first, group):
    blocks_dev, _, keys = weights.shape
    return pl.pallas_call(
        functools.partial(values_kernel, first, group),
        out_shape=held((blocks_dev * BLOCK, group * HEAD_SIZE)),
        in_specs=[VMEM] * (1 + len(value_parts)),
        out_specs=VMEM,
        compiler_params=params(16),
        cost_estimate=cost(4 * blocks_dev * BLOCK * group * keys * HEAD_SIZE, 1 << 20),
    )(weights, *value_parts)


def projection_kernel(places, width, fresh, last, weight_ref, *refs):
    refs = list(refs)
    total_ref = None if fresh else refs.pop(0)
    parts = refs[: len(places)]
    out_ref = refs[len(places)]
    columns = weight_ref.shape[1]
    tile = columns // 4 if last else columns
    me = lax.axis_index("head")
    copies = []
    for n in range(0, columns, tile):
        total = None if fresh else total_ref[:, n : n + tile]
        for (bits, offset), part in zip(places, parts):
            depth = part.shape[1]
            row = pl.multiple_of((me ^ bits) * width + offset, depth)
            term = jnp.dot(
                part[...],
                weight_ref[pl.ds(row, depth), n : n + tile],
                preferred_element_type=jnp.float32,
            )
            total = term if total is None else total + term
        if last:
            held_ref, sems = refs[len(places) + 1 :]
            held_ref[:, n : n + tile] = total.astype(held_ref.dtype)
            copy = pltpu.make_async_copy(
                held_ref.at[:, pl.ds(n, tile)], out_ref.at[:, pl.ds(n, tile)], sems.at[n // tile]
            )
            copy.start()
            copies.append(copy)
        else:
            out_ref[...] = total
    for copy in copies:
        copy.wait()


def projected(total, weight, width, places, parts, last=False):
    rows = parts[0].shape[0]
    columns = weight.shape[1]
    fresh = total is None
    operands = ([] if fresh else [total]) + parts
    shape = (rows, columns)
    depth = sum(part.shape[1] for part in parts)
    return pl.pallas_call(
        functools.partial(projection_kernel, places, width, fresh, last),
        out_shape=jax.ShapeDtypeStruct(shape, jnp.bfloat16) if last else held(shape, jnp.float32),
        in_specs=[VMEM] * (1 + len(operands)),
        out_specs=HBM if last else VMEM,
        scratch_shapes=[pltpu.VMEM(shape, jnp.bfloat16), pltpu.SemaphoreType.DMA((4,))]
        if last
        else [],
        compiler_params=params(8),
        cost_estimate=cost(8 * rows * depth * columns, 1 << 20),
    )(weight, *operands)


def gathered_over_ctx(part, steps):
    if len(steps) == 4:
        return [part] + [shifted(part, "ctx", step) for step in steps[1:]]
    whole = lax.all_gather(part, "ctx")
    return [whole[i] for i in range(len(steps))]


def on_device(queries, key_vectors, value_head_vectors, block_pattern, out_weight):
    heads_dev = queries.shape[1] // HEAD_SIZE
    count = lax.axis_size("ctx")
    steps = (0, 2, 1, 3) if count == 4 else tuple(range(count))
    barrier = lax.optimization_barrier
    keys, values = own_slices(key_vectors, value_head_vectors, queries.shape[1])
    key_parts = gathered_over_ctx(keys, steps)
    value_parts = gathered_over_ctx(values, steps)
    if count == 4:
        key_parts[2], queries = barrier((key_parts[2], queries))
    stacked, mask = stacked_of(queries, block_pattern, steps, count if count == 4 else None)
    weights = weights_of(stacked, mask, key_parts)
    if lax.axis_size("head") != 8:
        att = attended_of(weights, value_parts, 0, heads_dev)
        mixed = jnp.dot(
            lax.all_gather(att, "head", axis=1, tiled=True),
            out_weight,
            preferred_element_type=jnp.float32,
        )
        return mixed.astype(jnp.bfloat16)

    barrier = lax.optimization_barrier
    weight = pltpu.with_memory_space_constraint(out_weight, pltpu.VMEM)
    half = heads_dev // 2
    a = attended_of(weights, value_parts, 0, half)
    b = attended_of(weights, value_parts, half, half)
    xa = swapped(a, "head", 2)
    yb = swapped(b, "head", 4)
    xb = swapped(b, "head", 2)
    ya = swapped(a, "head", 4)
    a, b = barrier((a, b))
    sa = swapped(a, "head", 1)
    sb = swapped(b, "head", 1)
    width, half = heads_dev * HEAD_SIZE, heads_dev * HEAD_SIZE // 2
    mixed = projected(
        None, weight, width, ((0, 0), (0, half), (1, 0), (1, half)), [a, b, sa, sb]
    )
    xa, mixed = barrier((xa, mixed))
    da = swapped(xa, "head", 4)
    yb, mixed = barrier((yb, mixed))
    db = swapped(yb, "head", 2)
    xas, ybs = swapped(xa, "head", 1), swapped(yb, "head", 1)
    mixed = projected(
        mixed, weight, width, ((2, 0), (3, 0), (4, half), (5, half)), [xa, xas, yb, ybs]
    )
    xbs, yas = swapped(xb, "head", 1), swapped(ya, "head", 1)
    mixed = projected(
        mixed, weight, width, ((2, half), (3, half), (4, 0), (5, 0)), [xb, xbs, ya, yas]
    )
    da, mixed = barrier((da, mixed))
    das, dbs = swapped(da, "head", 1), swapped(db, "head", 1)
    mixed = projected(mixed, weight, width, ((6, 0), (6, half)), [da, db])
    return projected(mixed, weight, width, ((7, 0), (7, half)), [das, dbs], True)


def solution(mesh):
    return jax.shard_map(
        on_device,
        mesh=mesh,
        in_specs=(P("ctx", "head"), P("ctx", None), P("ctx", None), P(), P(None, "head")),
        out_specs=P("ctx", "head"),
        check_vma=False,
    )
```

```python
import functools
import math

import jax
import jax.numpy as jnp
from jax import lax
from jax.experimental import pallas as pl
from jax.experimental.pallas import tpu as pltpu
from jax.sharding import PartitionSpec as P

QUERY_HEADS = 64
KEY_VALUE_HEADS = 8
HEAD_SIZE = 128
BLOCK = 128
FAR = -1e30

SMEM = pl.BlockSpec(memory_space=pltpu.SMEM)
VMEM = pl.BlockSpec(memory_space=pltpu.VMEM)
HBM = pl.BlockSpec(memory_space=pltpu.HBM)


def params(mib):
    return pltpu.CompilerParams(vmem_limit_bytes=mib << 20)


def held(shape, dtype=jnp.bfloat16):
    return pltpu.VMEM(shape, dtype)


def in_hbm(value):
    return pltpu.with_memory_space_constraint(value, pltpu.HBM)


def cost(flops, moved):
    return pl.CostEstimate(flops=flops, bytes_accessed=moved, transcendentals=0)


def shifted(value, axis, steps):
    count = lax.axis_size(axis)
    return lax.ppermute(value, axis, [(source, (source + steps) % count) for source in range(count)])


def swapped(value, axis, bits):
    count = lax.axis_size(axis)
    return lax.ppermute(value, axis, [(source, source ^ bits) for source in range(count)])


def first_lane(shape):
    return lax.broadcasted_iota(jnp.int32, shape, 1) == 0


def slice_kernel(width, keys_ref, values_ref, own_keys_ref, own_values_ref, sems):
    heads = width // HEAD_SIZE
    head = lax.div(lax.axis_index("head") * heads, QUERY_HEADS // KEY_VALUE_HEADS)
    columns = pl.ds(pl.multiple_of(head * HEAD_SIZE, HEAD_SIZE), HEAD_SIZE)
    copies = [
        pltpu.make_async_copy(keys_ref.at[:, columns], own_keys_ref, sems.at[0]),
        pltpu.make_async_copy(values_ref.at[:, columns], own_values_ref, sems.at[1]),
    ]
    for copy in copies:
        copy.start()
    for copy in copies:
        copy.wait()


def own_slices(key_vectors, value_vectors, width):
    own = held((key_vectors.shape[0], HEAD_SIZE))
    return pl.pallas_call(
        functools.partial(slice_kernel, width),
        out_shape=[own, own],
        in_specs=[HBM] * 2,
        out_specs=[VMEM] * 2,
        scratch_shapes=[pltpu.SemaphoreType.DMA((2,))],
        compiler_params=params(8),
        cost_estimate=cost(0, 1 << 18),
    )(in_hbm(key_vectors), in_hbm(value_vectors))


def stack_kernel(steps, count, q_ref, pattern_ref, *refs):
    stacked_ref, mask_ref, table_ref, table_sem, sems = refs
    blocks_dev, rows, _ = stacked_ref.shape
    heads = rows // BLOCK
    table = pltpu.make_async_copy(pattern_ref, table_ref, table_sem)
    table.start()
    copies = []
    for a in range(blocks_dev):
        for h in range(heads):
            copies.append(
                pltpu.make_async_copy(
                    q_ref.at[pl.ds(a * BLOCK, BLOCK), pl.ds(h * HEAD_SIZE, HEAD_SIZE)],
                    stacked_ref.at[a, pl.ds(h * BLOCK, BLOCK)],
                    sems.at[a, h],
                )
            )
    for copy in copies:
        copy.start()
    table.wait()
    me = lax.axis_index("ctx")
    lane = first_lane((BLOCK, BLOCK))
    for a in range(blocks_dev):
        query_block = me * blocks_dev + a
        row = 0
        for step in steps:
            source = step if count is None else lax.rem(me + (count - step), count)
            for j in range(blocks_dev):
                key_block = source * blocks_dev + j
                on = (table_ref[query_block, key_block] == 1) | (query_block == key_block)
                mask_ref[a, row : row + BLOCK, :] = jnp.where(
                    lane, jnp.where(on, 0.0, FAR), 0.0
                ).astype(jnp.bfloat16)
                row += BLOCK
    for copy in copies:
        copy.wait()


def stacked_of(queries, block_pattern, steps, count):
    tok_dev, width = queries.shape
    blocks_dev, heads = tok_dev // BLOCK, width // HEAD_SIZE
    return pl.pallas_call(
        functools.partial(stack_kernel, steps, count),
        out_shape=[
            held((blocks_dev, heads * BLOCK, HEAD_SIZE)),
            held((blocks_dev, len(steps) * tok_dev, BLOCK)),
        ],
        in_specs=[HBM] * 2,
        out_specs=[VMEM] * 2,
        scratch_shapes=[
            pltpu.SMEM(block_pattern.shape, jnp.int32),
            pltpu.SemaphoreType.DMA(()),
            pltpu.SemaphoreType.DMA((blocks_dev, heads)),
        ],
        compiler_params=params(8),
        cost_estimate=cost(0, 1 << 20),
    )(in_hbm(queries), in_hbm(block_pattern))


def weights_kernel(q_ref, mask_ref, *refs):
    *key_refs, out_ref = refs
    blocks_dev, rows, _ = q_ref.shape
    group = min(rows, 512)
    exponent_scale = math.log2(math.e) / math.sqrt(HEAD_SIZE)
    keys = jnp.concatenate([ref[...] for ref in key_refs], axis=0)
    lane = jnp.where(first_lane((group, BLOCK)), 1.0, 0.0).astype(jnp.bfloat16)
    for a in range(blocks_dev):
        wide_keys = jnp.concatenate([keys, mask_ref[a]], axis=1)
        for first in range(0, rows, group):
            wide = jnp.concatenate([q_ref[a, first : first + group, :], lane], axis=1)
            scores = lax.dot_general(
                wide, wide_keys, (((1,), (1,)), ((), ())), preferred_element_type=jnp.float32
            )
            top = jnp.max(scores, axis=1, keepdims=True)
            out_ref[a, first : first + group, :] = jnp.exp2(
                (scores - top) * exponent_scale
            ).astype(jnp.bfloat16)


def weights_of(stacked, mask, key_parts):
    blocks_dev, rows, _ = stacked.shape
    keys = mask.shape[1]
    return pl.pallas_call(
        weights_kernel,
        out_shape=held((blocks_dev, rows, keys)),
        in_specs=[VMEM] * (2 + len(key_parts)),
        out_specs=VMEM,
        compiler_params=params(8 + (min(rows, 512) * keys * 16 >> 20)),
        cost_estimate=cost(8 * blocks_dev * rows * keys * HEAD_SIZE, 4 << 20),
    )(stacked, mask, *key_parts)


def values_kernel(first, group, weights_ref, *refs):
    value_refs, out_ref = refs[:-1], refs[-1]
    values = jnp.concatenate([ref[...] for ref in value_refs], axis=0)
    values = jnp.concatenate([values, jnp.ones_like(values)], axis=1)
    for a in range(weights_ref.shape[0]):
        summed = jnp.dot(
            weights_ref[a, first * BLOCK : (first + group) * BLOCK, :],
            values,
            preferred_element_type=jnp.float32,
        )
        result = (summed[:, :HEAD_SIZE] / summed[:, HEAD_SIZE:]).astype(jnp.bfloat16)
        for i in range(group):
            out_ref[a * BLOCK : (a + 1) * BLOCK, i * HEAD_SIZE : (i + 1) * HEAD_SIZE] = result[
                i * BLOCK : (i + 1) * BLOCK
            ]


def attended_of(weights, value_parts, first, group):
    blocks_dev, _, keys = weights.shape
    return pl.pallas_call(
        functools.partial(values_kernel, first, group),
        out_shape=held((blocks_dev * BLOCK, group * HEAD_SIZE)),
        in_specs=[VMEM] * (1 + len(value_parts)),
        out_specs=VMEM,
        compiler_params=params(16),
        cost_estimate=cost(4 * blocks_dev * BLOCK * group * keys * HEAD_SIZE, 1 << 20),
    )(weights, *value_parts)


def projection_kernel(places, width, fresh, last, weight_ref, *refs):
    refs = list(refs)
    total_ref = None if fresh else refs.pop(0)
    parts = refs[: len(places)]
    out_ref = refs[len(places)]
    columns = weight_ref.shape[1]
    tile = columns // 4 if last else columns
    me = lax.axis_index("head")
    copies = []
    for n in range(0, columns, tile):
        total = None if fresh else total_ref[:, n : n + tile]
        for (bits, offset), part in zip(places, parts):
            depth = part.shape[1]
            row = pl.multiple_of((me ^ bits) * width + offset, depth)
            term = jnp.dot(
                part[...],
                weight_ref[pl.ds(row, depth), n : n + tile],
                preferred_element_type=jnp.float32,
            )
            total = term if total is None else total + term
        if last:
            held_ref, sems = refs[len(places) + 1 :]
            held_ref[:, n : n + tile] = total.astype(held_ref.dtype)
            copy = pltpu.make_async_copy(
                held_ref.at[:, pl.ds(n, tile)], out_ref.at[:, pl.ds(n, tile)], sems.at[n // tile]
            )
            copy.start()
            copies.append(copy)
        else:
            out_ref[...] = total
    for copy in copies:
        copy.wait()


def projected(total, weight, width, places, parts, last=False):
    rows = parts[0].shape[0]
    columns = weight.shape[1]
    fresh = total is None
    operands = ([] if fresh else [total]) + parts
    shape = (rows, columns)
    depth = sum(part.shape[1] for part in parts)
    return pl.pallas_call(
        functools.partial(projection_kernel, places, width, fresh, last),
        out_shape=jax.ShapeDtypeStruct(shape, jnp.bfloat16) if last else held(shape, jnp.float32),
        in_specs=[VMEM] * (1 + len(operands)),
        out_specs=HBM if last else VMEM,
        scratch_shapes=[pltpu.VMEM(shape, jnp.bfloat16), pltpu.SemaphoreType.DMA((4,))]
        if last
        else [],
        compiler_params=params(8),
        cost_estimate=cost(8 * rows * depth * columns, 1 << 20),
    )(weight, *operands)


def gathered_over_ctx(part, steps):
    if len(steps) == 4:
        return [part] + [shifted(part, "ctx", step) for step in steps[1:]]
    whole = lax.all_gather(part, "ctx")
    return [whole[i] for i in range(len(steps))]


def on_device(queries, key_vectors, value_head_vectors, block_pattern, out_weight):
    heads_dev = queries.shape[1] // HEAD_SIZE
    count = lax.axis_size("ctx")
    steps = (0, 2, 1, 3) if count == 4 else tuple(range(count))
    barrier = lax.optimization_barrier
    keys, values = own_slices(key_vectors, value_head_vectors, queries.shape[1])
    key_parts = gathered_over_ctx(keys, steps)
    value_parts = gathered_over_ctx(values, steps)
    if count == 4:
        key_parts[2], queries = barrier((key_parts[2], queries))
    stacked, mask = stacked_of(queries, block_pattern, steps, count if count == 4 else None)
    weights = weights_of(stacked, mask, key_parts)
    if lax.axis_size("head") != 8:
        att = attended_of(weights, value_parts, 0, heads_dev)
        mixed = jnp.dot(
            lax.all_gather(att, "head", axis=1, tiled=True),
            out_weight,
            preferred_element_type=jnp.float32,
        )
        return mixed.astype(jnp.bfloat16)

    barrier = lax.optimization_barrier
    weight = pltpu.with_memory_space_constraint(out_weight, pltpu.VMEM)
    half = heads_dev // 2
    a = attended_of(weights, value_parts, 0, half)
    b = attended_of(weights, value_parts, half, half)
    xa = swapped(a, "head", 2)
    yb = swapped(b, "head", 4)
    xb = swapped(b, "head", 2)
    ya = swapped(a, "head", 4)
    a, b = barrier((a, b))
    sa = swapped(a, "head", 1)
    sb = swapped(b, "head", 1)
    width, half = heads_dev * HEAD_SIZE, heads_dev * HEAD_SIZE // 2
    mixed = projected(
        None, weight, width, ((0, 0), (0, half), (1, 0), (1, half)), [a, b, sa, sb]
    )
    xa, yb, mixed = barrier((xa, yb, mixed))
    da = swapped(xa, "head", 4)
    yb_late, _ = barrier((yb, ya))
    db = swapped(yb_late, "head", 2)
    xas, ybs = swapped(xa, "head", 1), swapped(yb, "head", 1)
    mixed = projected(
        mixed, weight, width, ((2, 0), (3, 0), (4, half), (5, half)), [xa, xas, yb, ybs]
    )
    xbs, yas = swapped(xb, "head", 1), swapped(ya, "head", 1)
    mixed = projected(
        mixed, weight, width, ((2, half), (3, half), (4, 0), (5, 0)), [xb, xbs, ya, yas]
    )
    da, mixed = barrier((da, mixed))
    das, dbs = swapped(da, "head", 1), swapped(db, "head", 1)
    mixed = projected(mixed, weight, width, ((6, 0), (6, half)), [da, db])
    return projected(mixed, weight, width, ((7, 0), (7, half)), [das, dbs], True)


def solution(mesh):
    return jax.shard_map(
        on_device,
        mesh=mesh,
        in_specs=(P("ctx", "head"), P("ctx", None), P("ctx", None), P(), P(None, "head")),
        out_specs=P("ctx", "head"),
        check_vma=False,
    )
```

```python
import functools
import math

import jax
import jax.numpy as jnp
from jax import lax
from jax.experimental import pallas as pl
from jax.experimental.pallas import tpu as pltpu
from jax.sharding import PartitionSpec as P

QUERY_HEADS = 64
KEY_VALUE_HEADS = 8
HEAD_SIZE = 128
BLOCK = 128
FAR = -1e30

SMEM = pl.BlockSpec(memory_space=pltpu.SMEM)
VMEM = pl.BlockSpec(memory_space=pltpu.VMEM)
HBM = pl.BlockSpec(memory_space=pltpu.HBM)


def params(mib):
    return pltpu.CompilerParams(vmem_limit_bytes=mib << 20)


def held(shape, dtype=jnp.bfloat16):
    return pltpu.VMEM(shape, dtype)


def in_hbm(value):
    return pltpu.with_memory_space_constraint(value, pltpu.HBM)


def cost(flops, moved):
    return pl.CostEstimate(flops=flops, bytes_accessed=moved, transcendentals=0)


def shifted(value, axis, steps):
    count = lax.axis_size(axis)
    return lax.ppermute(value, axis, [(source, (source + steps) % count) for source in range(count)])


def swapped(value, axis, bits):
    count = lax.axis_size(axis)
    return lax.ppermute(value, axis, [(source, source ^ bits) for source in range(count)])


def first_lane(shape):
    return lax.broadcasted_iota(jnp.int32, shape, 1) == 0


def slice_kernel(width, keys_ref, values_ref, own_keys_ref, own_values_ref, sems):
    heads = width // HEAD_SIZE
    head = lax.div(lax.axis_index("head") * heads, QUERY_HEADS // KEY_VALUE_HEADS)
    columns = pl.ds(pl.multiple_of(head * HEAD_SIZE, HEAD_SIZE), HEAD_SIZE)
    copies = [
        pltpu.make_async_copy(keys_ref.at[:, columns], own_keys_ref, sems.at[0]),
        pltpu.make_async_copy(values_ref.at[:, columns], own_values_ref, sems.at[1]),
    ]
    for copy in copies:
        copy.start()
    for copy in copies:
        copy.wait()


def own_slices(key_vectors, value_vectors, width):
    own = held((key_vectors.shape[0], HEAD_SIZE))
    return pl.pallas_call(
        functools.partial(slice_kernel, width),
        out_shape=[own, own],
        in_specs=[HBM] * 2,
        out_specs=[VMEM] * 2,
        scratch_shapes=[pltpu.SemaphoreType.DMA((2,))],
        compiler_params=params(8),
        cost_estimate=cost(0, 1 << 18),
    )(in_hbm(key_vectors), in_hbm(value_vectors))


def stack_kernel(steps, count, q_ref, pattern_ref, *refs):
    stacked_ref, mask_ref, table_ref, table_sem, sems = refs
    blocks_dev, rows, _ = stacked_ref.shape
    heads = rows // BLOCK
    table = pltpu.make_async_copy(pattern_ref, table_ref, table_sem)
    table.start()
    copies = []
    for a in range(blocks_dev):
        for h in range(heads):
            copies.append(
                pltpu.make_async_copy(
                    q_ref.at[pl.ds(a * BLOCK, BLOCK), pl.ds(h * HEAD_SIZE, HEAD_SIZE)],
                    stacked_ref.at[a, pl.ds(h * BLOCK, BLOCK)],
                    sems.at[a, h],
                )
            )
    for copy in copies:
        copy.start()
    table.wait()
    me = lax.axis_index("ctx")
    lane = first_lane((BLOCK, BLOCK))
    for a in range(blocks_dev):
        query_block = me * blocks_dev + a
        row = 0
        for step in steps:
            source = step if count is None else lax.rem(me + (count - step), count)
            for j in range(blocks_dev):
                key_block = source * blocks_dev + j
                on = (table_ref[query_block, key_block] == 1) | (query_block == key_block)
                mask_ref[a, row : row + BLOCK, :] = jnp.where(
                    lane, jnp.where(on, 0.0, FAR), 0.0
                ).astype(jnp.bfloat16)
                row += BLOCK
    for copy in copies:
        copy.wait()


def stacked_of(queries, block_pattern, steps, count):
    tok_dev, width = queries.shape
    blocks_dev, heads = tok_dev // BLOCK, width // HEAD_SIZE
    return pl.pallas_call(
        functools.partial(stack_kernel, steps, count),
        out_shape=[
            held((blocks_dev, heads * BLOCK, HEAD_SIZE)),
            held((blocks_dev, len(steps) * tok_dev, BLOCK)),
        ],
        in_specs=[HBM] * 2,
        out_specs=[VMEM] * 2,
        scratch_shapes=[
            pltpu.SMEM(block_pattern.shape, jnp.int32),
            pltpu.SemaphoreType.DMA(()),
            pltpu.SemaphoreType.DMA((blocks_dev, heads)),
        ],
        compiler_params=params(8),
        cost_estimate=cost(0, 1 << 20),
    )(in_hbm(queries), in_hbm(block_pattern))


def weights_kernel(q_ref, mask_ref, *refs):
    *key_refs, out_ref = refs
    blocks_dev, rows, _ = q_ref.shape
    group = min(rows, 512)
    exponent_scale = math.log2(math.e) / math.sqrt(HEAD_SIZE)
    keys = jnp.concatenate([ref[...] for ref in key_refs], axis=0)
    lane = jnp.where(first_lane((group, BLOCK)), 1.0, 0.0).astype(jnp.bfloat16)
    for a in range(blocks_dev):
        wide_keys = jnp.concatenate([keys, mask_ref[a]], axis=1)
        for first in range(0, rows, group):
            wide = jnp.concatenate([q_ref[a, first : first + group, :], lane], axis=1)
            scores = lax.dot_general(
                wide, wide_keys, (((1,), (1,)), ((), ())), preferred_element_type=jnp.float32
            )
            top = jnp.max(scores, axis=1, keepdims=True)
            out_ref[a, first : first + group, :] = jnp.exp2(
                (scores - top) * exponent_scale
            ).astype(jnp.bfloat16)


def weights_of(stacked, mask, key_parts):
    blocks_dev, rows, _ = stacked.shape
    keys = mask.shape[1]
    return pl.pallas_call(
        weights_kernel,
        out_shape=held((blocks_dev, rows, keys)),
        in_specs=[VMEM] * (2 + len(key_parts)),
        out_specs=VMEM,
        compiler_params=params(8 + (min(rows, 512) * keys * 16 >> 20)),
        cost_estimate=cost(400 * blocks_dev * rows * keys * HEAD_SIZE, 4 << 20),
    )(stacked, mask, *key_parts)


def values_kernel(count, weights_ref, *refs):
    values = jnp.concatenate([ref[...] for ref in refs[:count]], axis=0)
    values = jnp.concatenate([values, jnp.ones_like(values)], axis=1)
    whole_ref, *piece_refs = refs[count:]
    blocks_dev, rows, _ = weights_ref.shape
    heads = rows // BLOCK
    pieces = max(1, len(piece_refs))
    group = heads // pieces
    for piece in range(pieces):
        for a in range(blocks_dev):
            first = piece * group
            summed = jnp.dot(
                weights_ref[a, first * BLOCK : (first + group) * BLOCK, :],
                values,
                preferred_element_type=jnp.float32,
            )
            result = (summed[:, :HEAD_SIZE] / summed[:, HEAD_SIZE:]).astype(jnp.bfloat16)
            for i in range(group):
                part = result[i * BLOCK : (i + 1) * BLOCK]
                tokens = slice(a * BLOCK, (a + 1) * BLOCK)
                column = (first + i) * HEAD_SIZE
                whole_ref[tokens, column : column + HEAD_SIZE] = part
                if piece_refs:
                    column = i * HEAD_SIZE
                    piece_refs[piece][tokens, column : column + HEAD_SIZE] = part


def attended_of(weights, value_parts, pieces):
    blocks_dev, rows, keys = weights.shape
    tokens, width = blocks_dev * BLOCK, rows // BLOCK * HEAD_SIZE
    shapes = [held((tokens, width))] + [held((tokens, width // 2))] * pieces
    return pl.pallas_call(
        functools.partial(values_kernel, len(value_parts)),
        out_shape=shapes,
        in_specs=[VMEM] * (1 + len(value_parts)),
        out_specs=[VMEM] * len(shapes),
        compiler_params=params(16),
        cost_estimate=cost(400 * tokens * width * keys, 1 << 20),
    )(weights, *value_parts)


def projection_kernel(places, width, fresh, last, weight_ref, *refs):
    refs = list(refs)
    total_ref = None if fresh else refs.pop(0)
    parts = refs[: len(places)]
    out_ref = refs[len(places)]
    columns = weight_ref.shape[1]
    tile = columns // 4 if last else columns
    me = lax.axis_index("head")
    copies = []
    for n in range(0, columns, tile):
        total = None if fresh else total_ref[:, n : n + tile]
        for place, part in zip(places, parts):
            several = place if isinstance(place[0], tuple) else (place,)
            rows = out_ref.shape[0]
            for index, (bits, offset) in enumerate(several):
                depth = part.shape[1]
                row = pl.multiple_of((me ^ bits) * width + offset, HEAD_SIZE)
                term = jnp.dot(
                    part[index * rows : (index + 1) * rows, :],
                    weight_ref[pl.ds(row, depth), n : n + tile],
                    preferred_element_type=jnp.float32,
                )
                total = term if total is None else total + term
        if last:
            held_ref, sems = refs[len(places) + 1 :]
            held_ref[:, n : n + tile] = total.astype(held_ref.dtype)
            copy = pltpu.make_async_copy(
                held_ref.at[:, pl.ds(n, tile)], out_ref.at[:, pl.ds(n, tile)], sems.at[n // tile]
            )
            copy.start()
            copies.append(copy)
        else:
            out_ref[...] = total
    for copy in copies:
        copy.wait()


def projected(total, weight, width, places, parts, last=False):
    rows = parts[0].shape[0]
    columns = weight.shape[1]
    fresh = total is None
    operands = ([] if fresh else [total]) + parts
    shape = (rows, columns)
    depth = sum(part.shape[1] for part in parts)
    return pl.pallas_call(
        functools.partial(projection_kernel, places, width, fresh, last),
        out_shape=jax.ShapeDtypeStruct(shape, jnp.bfloat16) if last else held(shape, jnp.float32),
        in_specs=[VMEM] * (1 + len(operands)),
        out_specs=HBM if last else VMEM,
        scratch_shapes=[pltpu.VMEM(shape, jnp.bfloat16), pltpu.SemaphoreType.DMA((4,))]
        if last
        else [],
        compiler_params=params(8),
        cost_estimate=cost(8 * rows * depth * columns, 1 << 20),
    )(weight, *operands)


def gathered_over_ctx(part, steps):
    if len(steps) == 4:
        return [part] + [shifted(part, "ctx", step) for step in steps[1:]]
    whole = lax.all_gather(part, "ctx")
    return [whole[i] for i in range(len(steps))]


def on_device(queries, key_vectors, value_head_vectors, block_pattern, out_weight):
    heads_dev = queries.shape[1] // HEAD_SIZE
    count = lax.axis_size("ctx")
    steps = (0, 2, 1, 3) if count == 4 else tuple(range(count))
    barrier = lax.optimization_barrier
    keys, values = own_slices(key_vectors, value_head_vectors, queries.shape[1])
    key_parts = gathered_over_ctx(keys, steps)
    value_parts = gathered_over_ctx(values, steps)
    if count == 4:
        key_parts[2], queries = barrier((key_parts[2], queries))
    stacked, mask = stacked_of(queries, block_pattern, steps, count if count == 4 else None)
    weights = weights_of(stacked, mask, key_parts)
    if lax.axis_size("head") != 8:
        (att,) = attended_of(weights, value_parts, 0)
        mixed = jnp.dot(
            lax.all_gather(att, "head", axis=1, tiled=True),
            out_weight,
            preferred_element_type=jnp.float32,
        )
        return mixed.astype(jnp.bfloat16)

    barrier = lax.optimization_barrier
    weight = pltpu.with_memory_space_constraint(out_weight, pltpu.VMEM)
    own, a, b = attended_of(weights, value_parts, 2)
    width, half = heads_dev * HEAD_SIZE, heads_dev * HEAD_SIZE // 2
    xa = swapped(a, "head", 2)
    yb = swapped(b, "head", 4)
    xb = swapped(b, "head", 2)
    ya = swapped(a, "head", 4)
    sibling = swapped(own, "head", 1)
    mixed = projected(None, weight, width, ((0, 0), (1, 0)), [own, sibling])
    da = swapped(xa, "head", 4)
    yb, mixed = barrier((yb, mixed))
    db = swapped(yb, "head", 2)
    xb, ya, mixed = barrier((xb, ya, mixed))
    xas = swapped(xa, "head", 1)
    mixed = projected(mixed, weight, width, ((2, 0), (2, half), (3, 0)), [xa, xb, xas])
    ybs = swapped(yb, "head", 1)
    xbs = swapped(xb, "head", 1)
    yas = swapped(ya, "head", 1)
    mixed = projected(mixed, weight, width, ((4, 0), (4, half), (5, half), (3, half), (5, 0)), [ya, yb, ybs, xbs, yas])
    da, mixed = barrier((da, mixed))
    da_s, db_s = swapped(da, "head", 1), swapped(db, "head", 1)
    mixed = projected(mixed, weight, width, ((6, 0), (6, half)), [da, db])
    return projected(mixed, weight, width, ((7, 0), (7, half)), [da_s, db_s], True)


def solution(mesh):
    return jax.shard_map(
        on_device,
        mesh=mesh,
        in_specs=(P("ctx", "head"), P("ctx", None), P("ctx", None), P(), P(None, "head")),
        out_specs=P("ctx", "head"),
        check_vma=False,
    )
```

```python
import functools
import math

import jax
import jax.numpy as jnp
from jax import lax
from jax.experimental import pallas as pl
from jax.experimental.pallas import tpu as pltpu
from jax.sharding import PartitionSpec as P

QUERY_HEADS = 64
KEY_VALUE_HEADS = 8
HEAD_SIZE = 128
BLOCK = 128
FAR = -1e30

SMEM = pl.BlockSpec(memory_space=pltpu.SMEM)
VMEM = pl.BlockSpec(memory_space=pltpu.VMEM)
HBM = pl.BlockSpec(memory_space=pltpu.HBM)


def params(mib):
    return pltpu.CompilerParams(vmem_limit_bytes=mib << 20)


def held(shape, dtype=jnp.bfloat16):
    return pltpu.VMEM(shape, dtype)


def in_hbm(value):
    return pltpu.with_memory_space_constraint(value, pltpu.HBM)


def cost(flops, moved):
    return pl.CostEstimate(flops=flops, bytes_accessed=moved, transcendentals=0)


def shifted(value, axis, steps):
    count = lax.axis_size(axis)
    return lax.ppermute(value, axis, [(source, (source + steps) % count) for source in range(count)])


def swapped(value, axis, bits):
    count = lax.axis_size(axis)
    return lax.ppermute(value, axis, [(source, source ^ bits) for source in range(count)])


def first_lane(shape):
    return lax.broadcasted_iota(jnp.int32, shape, 1) == 0


def slice_kernel(width, keys_ref, values_ref, own_keys_ref, own_values_ref, sems):
    heads = width // HEAD_SIZE
    head = lax.div(lax.axis_index("head") * heads, QUERY_HEADS // KEY_VALUE_HEADS)
    columns = pl.ds(pl.multiple_of(head * HEAD_SIZE, HEAD_SIZE), HEAD_SIZE)
    copies = [
        pltpu.make_async_copy(keys_ref.at[:, columns], own_keys_ref, sems.at[0]),
        pltpu.make_async_copy(values_ref.at[:, columns], own_values_ref, sems.at[1]),
    ]
    for copy in copies:
        copy.start()
    for copy in copies:
        copy.wait()


def own_slices(key_vectors, value_vectors, width):
    own = held((key_vectors.shape[0], HEAD_SIZE))
    return pl.pallas_call(
        functools.partial(slice_kernel, width),
        out_shape=[own, own],
        in_specs=[HBM] * 2,
        out_specs=[VMEM] * 2,
        scratch_shapes=[pltpu.SemaphoreType.DMA((2,))],
        compiler_params=params(8),
        cost_estimate=cost(0, 1 << 18),
    )(in_hbm(key_vectors), in_hbm(value_vectors))


def stack_kernel(steps, count, q_ref, pattern_ref, *refs):
    stacked_ref, mask_ref, table_ref, table_sem, sems = refs
    blocks_dev, rows, _ = stacked_ref.shape
    heads = rows // BLOCK
    table = pltpu.make_async_copy(pattern_ref, table_ref, table_sem)
    table.start()
    copies = []
    for a in range(blocks_dev):
        for h in range(heads):
            copies.append(
                pltpu.make_async_copy(
                    q_ref.at[pl.ds(a * BLOCK, BLOCK), pl.ds(h * HEAD_SIZE, HEAD_SIZE)],
                    stacked_ref.at[a, pl.ds(h * BLOCK, BLOCK)],
                    sems.at[a, h],
                )
            )
    for copy in copies:
        copy.start()
    table.wait()
    me = lax.axis_index("ctx")
    lane = first_lane((BLOCK, BLOCK))
    for a in range(blocks_dev):
        query_block = me * blocks_dev + a
        row = 0
        for step in steps:
            source = step if count is None else lax.rem(me + (count - step), count)
            for j in range(blocks_dev):
                key_block = source * blocks_dev + j
                on = (table_ref[query_block, key_block] == 1) | (query_block == key_block)
                mask_ref[a, row : row + BLOCK, :] = jnp.where(
                    lane, jnp.where(on, 0.0, FAR), 0.0
                ).astype(jnp.bfloat16)
                row += BLOCK
    for copy in copies:
        copy.wait()


def stacked_of(queries, block_pattern, steps, count):
    tok_dev, width = queries.shape
    blocks_dev, heads = tok_dev // BLOCK, width // HEAD_SIZE
    return pl.pallas_call(
        functools.partial(stack_kernel, steps, count),
        out_shape=[
            held((blocks_dev, heads * BLOCK, HEAD_SIZE)),
            held((blocks_dev, len(steps) * tok_dev, BLOCK)),
        ],
        in_specs=[HBM] * 2,
        out_specs=[VMEM] * 2,
        scratch_shapes=[
            pltpu.SMEM(block_pattern.shape, jnp.int32),
            pltpu.SemaphoreType.DMA(()),
            pltpu.SemaphoreType.DMA((blocks_dev, heads)),
        ],
        compiler_params=params(8),
        cost_estimate=cost(0, 1 << 20),
    )(in_hbm(queries), in_hbm(block_pattern))


def weights_kernel(q_ref, mask_ref, *refs):
    *key_refs, out_ref = refs
    blocks_dev, rows, _ = q_ref.shape
    group = min(rows, 512)
    exponent_scale = math.log2(math.e) / math.sqrt(HEAD_SIZE)
    keys = jnp.concatenate([ref[...] for ref in key_refs], axis=0)
    lane = jnp.where(first_lane((group, BLOCK)), 1.0, 0.0).astype(jnp.bfloat16)
    for a in range(blocks_dev):
        wide_keys = jnp.concatenate([keys, mask_ref[a]], axis=1)
        for first in range(0, rows, group):
            wide = jnp.concatenate([q_ref[a, first : first + group, :], lane], axis=1)
            scores = lax.dot_general(
                wide, wide_keys, (((1,), (1,)), ((), ())), preferred_element_type=jnp.float32
            )
            top = jnp.max(scores, axis=1, keepdims=True)
            out_ref[a, first : first + group, :] = jnp.exp2(
                (scores - top) * exponent_scale
            ).astype(jnp.bfloat16)


def weights_of(stacked, mask, key_parts):
    blocks_dev, rows, _ = stacked.shape
    keys = mask.shape[1]
    return pl.pallas_call(
        weights_kernel,
        out_shape=held((blocks_dev, rows, keys)),
        in_specs=[VMEM] * (2 + len(key_parts)),
        out_specs=VMEM,
        compiler_params=params(8 + (min(rows, 512) * keys * 16 >> 20)),
        cost_estimate=cost(400 * blocks_dev * rows * keys * HEAD_SIZE, 4 << 20),
    )(stacked, mask, *key_parts)


def values_kernel(count, weights_ref, *refs):
    values = jnp.concatenate([ref[...] for ref in refs[:count]], axis=0)
    values = jnp.concatenate([values, jnp.ones_like(values)], axis=1)
    whole_ref, *piece_refs = refs[count:]
    blocks_dev, rows, _ = weights_ref.shape
    heads = rows // BLOCK
    pieces = max(1, len(piece_refs))
    group = heads // pieces
    for piece in range(pieces):
        for a in range(blocks_dev):
            first = piece * group
            summed = jnp.dot(
                weights_ref[a, first * BLOCK : (first + group) * BLOCK, :],
                values,
                preferred_element_type=jnp.float32,
            )
            result = (summed[:, :HEAD_SIZE] / summed[:, HEAD_SIZE:]).astype(jnp.bfloat16)
            for i in range(group):
                part = result[i * BLOCK : (i + 1) * BLOCK]
                tokens = slice(a * BLOCK, (a + 1) * BLOCK)
                column = (first + i) * HEAD_SIZE
                whole_ref[tokens, column : column + HEAD_SIZE] = part
                if piece_refs:
                    column = i * HEAD_SIZE
                    piece_refs[piece][tokens, column : column + HEAD_SIZE] = part


def attended_of(weights, value_parts, pieces):
    blocks_dev, rows, keys = weights.shape
    tokens, width = blocks_dev * BLOCK, rows // BLOCK * HEAD_SIZE
    shapes = [held((tokens, width))] + [held((tokens, width // 2))] * pieces
    return pl.pallas_call(
        functools.partial(values_kernel, len(value_parts)),
        out_shape=shapes,
        in_specs=[VMEM] * (1 + len(value_parts)),
        out_specs=[VMEM] * len(shapes),
        compiler_params=params(16),
        cost_estimate=cost(400 * tokens * width * keys, 1 << 20),
    )(weights, *value_parts)


def projection_kernel(places, width, fresh, last, weight_ref, *refs):
    refs = list(refs)
    total_ref = None if fresh else refs.pop(0)
    parts = refs[: len(places)]
    out_ref = refs[len(places)]
    columns = weight_ref.shape[1]
    tile = columns // 4 if last else columns
    me = lax.axis_index("head")
    copies = []
    for n in range(0, columns, tile):
        total = None if fresh else total_ref[:, n : n + tile]
        for place, part in zip(places, parts):
            several = place if isinstance(place[0], tuple) else (place,)
            rows = out_ref.shape[0]
            for index, (bits, offset) in enumerate(several):
                depth = part.shape[1]
                row = pl.multiple_of((me ^ bits) * width + offset, HEAD_SIZE)
                term = jnp.dot(
                    part[index * rows : (index + 1) * rows, :],
                    weight_ref[pl.ds(row, depth), n : n + tile],
                    preferred_element_type=jnp.float32,
                )
                total = term if total is None else total + term
        if last:
            held_ref, sems = refs[len(places) + 1 :]
            held_ref[:, n : n + tile] = total.astype(held_ref.dtype)
            copy = pltpu.make_async_copy(
                held_ref.at[:, pl.ds(n, tile)], out_ref.at[:, pl.ds(n, tile)], sems.at[n // tile]
            )
            copy.start()
            copies.append(copy)
        else:
            out_ref[...] = total
    for copy in copies:
        copy.wait()


def projected(total, weight, width, places, parts, last=False):
    rows = parts[0].shape[0]
    columns = weight.shape[1]
    fresh = total is None
    operands = ([] if fresh else [total]) + parts
    shape = (rows, columns)
    depth = sum(part.shape[1] for part in parts)
    return pl.pallas_call(
        functools.partial(projection_kernel, places, width, fresh, last),
        out_shape=jax.ShapeDtypeStruct(shape, jnp.bfloat16) if last else held(shape, jnp.float32),
        in_specs=[VMEM] * (1 + len(operands)),
        out_specs=HBM if last else VMEM,
        scratch_shapes=[pltpu.VMEM(shape, jnp.bfloat16), pltpu.SemaphoreType.DMA((4,))]
        if last
        else [],
        compiler_params=params(8),
        cost_estimate=cost(8 * rows * depth * columns, 1 << 20),
    )(weight, *operands)


def gathered_over_ctx(part, steps):
    if len(steps) == 4:
        return [part] + [shifted(part, "ctx", step) for step in steps[1:]]
    whole = lax.all_gather(part, "ctx")
    return [whole[i] for i in range(len(steps))]


def on_device(queries, key_vectors, value_head_vectors, block_pattern, out_weight):
    heads_dev = queries.shape[1] // HEAD_SIZE
    count = lax.axis_size("ctx")
    steps = (0, 2, 1, 3) if count == 4 else tuple(range(count))
    barrier = lax.optimization_barrier
    keys, values = own_slices(key_vectors, value_head_vectors, queries.shape[1])
    key_parts = gathered_over_ctx(keys, steps)
    value_parts = gathered_over_ctx(values, steps)
    if count == 4:
        key_parts[2], queries = barrier((key_parts[2], queries))
    stacked, mask = stacked_of(queries, block_pattern, steps, count if count == 4 else None)
    weights = weights_of(stacked, mask, key_parts)
    if lax.axis_size("head") != 8:
        (att,) = attended_of(weights, value_parts, 0)
        mixed = jnp.dot(
            lax.all_gather(att, "head", axis=1, tiled=True),
            out_weight,
            preferred_element_type=jnp.float32,
        )
        return mixed.astype(jnp.bfloat16)

    barrier = lax.optimization_barrier
    weight = pltpu.with_memory_space_constraint(out_weight, pltpu.VMEM)
    own, a, b = attended_of(weights, value_parts, 2)
    width, half = heads_dev * HEAD_SIZE, heads_dev * HEAD_SIZE // 2
    xa = swapped(a, "head", 2)
    yb = swapped(b, "head", 4)
    xb = swapped(b, "head", 2)
    ya = swapped(a, "head", 4)
    sa, sb = swapped(a, "head", 1), swapped(b, "head", 1)
    mixed = projected(None, weight, width, ((0, 0), (0, half), (1, 0), (1, half)), [a, b, sa, sb])
    xa, mixed = barrier((xa, mixed))
    da = swapped(xa, "head", 4)
    yb, mixed = barrier((yb, mixed))
    db = swapped(yb, "head", 2)
    xb, ya, mixed = barrier((xb, ya, mixed))
    xas = swapped(xa, "head", 1)
    ybs = swapped(yb, "head", 1)
    mixed = projected(mixed, weight, width, ((2, 0), (3, 0), (4, half), (5, half)), [xa, xas, yb, ybs])
    xbs = swapped(xb, "head", 1)
    yas = swapped(ya, "head", 1)
    mixed = projected(mixed, weight, width, ((2, half), (4, 0), (3, half), (5, 0)), [xb, ya, xbs, yas])
    da, mixed = barrier((da, mixed))
    da_s, db_s = swapped(da, "head", 1), swapped(db, "head", 1)
    mixed = projected(mixed, weight, width, ((6, 0), (6, half), (7, 0)), [da, db, da_s])
    return projected(mixed, weight, width, ((7, half),), [db_s], True)


def solution(mesh):
    return jax.shard_map(
        on_device,
        mesh=mesh,
        in_specs=(P("ctx", "head"), P("ctx", None), P("ctx", None), P(), P(None, "head")),
        out_specs=P("ctx", "head"),
        check_vma=False,
    )
```

```python
import functools
import math

import jax
import jax.numpy as jnp
from jax import lax
from jax.experimental import pallas as pl
from jax.experimental.pallas import tpu as pltpu
from jax.sharding import PartitionSpec as P

QUERY_HEADS = 64
KEY_VALUE_HEADS = 8
HEAD_SIZE = 128
BLOCK = 128
FAR = -1e30

SMEM = pl.BlockSpec(memory_space=pltpu.SMEM)
VMEM = pl.BlockSpec(memory_space=pltpu.VMEM)
HBM = pl.BlockSpec(memory_space=pltpu.HBM)


def params(mib):
    return pltpu.CompilerParams(vmem_limit_bytes=mib << 20)


def held(shape, dtype=jnp.bfloat16):
    return pltpu.VMEM(shape, dtype)


def in_hbm(value):
    return pltpu.with_memory_space_constraint(value, pltpu.HBM)


def cost(flops, moved):
    return pl.CostEstimate(flops=flops, bytes_accessed=moved, transcendentals=0)


def shifted(value, axis, steps):
    count = lax.axis_size(axis)
    return lax.ppermute(value, axis, [(source, (source + steps) % count) for source in range(count)])


def swapped(value, axis, bits):
    count = lax.axis_size(axis)
    return lax.ppermute(value, axis, [(source, source ^ bits) for source in range(count)])


def first_lane(shape):
    return lax.broadcasted_iota(jnp.int32, shape, 1) == 0


def slice_kernel(width, keys_ref, values_ref, own_keys_ref, own_values_ref, sems):
    heads = width // HEAD_SIZE
    head = lax.div(lax.axis_index("head") * heads, QUERY_HEADS // KEY_VALUE_HEADS)
    columns = pl.ds(pl.multiple_of(head * HEAD_SIZE, HEAD_SIZE), HEAD_SIZE)
    copies = [
        pltpu.make_async_copy(keys_ref.at[:, columns], own_keys_ref, sems.at[0]),
        pltpu.make_async_copy(values_ref.at[:, columns], own_values_ref, sems.at[1]),
    ]
    for copy in copies:
        copy.start()
    for copy in copies:
        copy.wait()


def own_slices(key_vectors, value_vectors, width):
    own = held((key_vectors.shape[0], HEAD_SIZE))
    return pl.pallas_call(
        functools.partial(slice_kernel, width),
        out_shape=[own, own],
        in_specs=[HBM] * 2,
        out_specs=[VMEM] * 2,
        scratch_shapes=[pltpu.SemaphoreType.DMA((2,))],
        compiler_params=params(8),
        cost_estimate=cost(0, 1 << 18),
    )(in_hbm(key_vectors), in_hbm(value_vectors))


def stack_kernel(steps, count, q_ref, pattern_ref, *refs):
    stacked_ref, mask_ref, table_ref, table_sem, sems = refs
    blocks_dev, rows, _ = stacked_ref.shape
    heads = rows // BLOCK
    table = pltpu.make_async_copy(pattern_ref, table_ref, table_sem)
    table.start()
    copies = []
    for a in range(blocks_dev):
        for h in range(heads):
            copies.append(
                pltpu.make_async_copy(
                    q_ref.at[pl.ds(a * BLOCK, BLOCK), pl.ds(h * HEAD_SIZE, HEAD_SIZE)],
                    stacked_ref.at[a, pl.ds(h * BLOCK, BLOCK)],
                    sems.at[a, h],
                )
            )
    for copy in copies:
        copy.start()
    table.wait()
    me = lax.axis_index("ctx")
    lane = first_lane((BLOCK, BLOCK))
    for a in range(blocks_dev):
        query_block = me * blocks_dev + a
        row = 0
        for step in steps:
            source = step if count is None else lax.rem(me + (count - step), count)
            for j in range(blocks_dev):
                key_block = source * blocks_dev + j
                on = (table_ref[query_block, key_block] == 1) | (query_block == key_block)
                mask_ref[a, row : row + BLOCK, :] = jnp.where(
                    lane, jnp.where(on, 0.0, FAR), 0.0
                ).astype(jnp.bfloat16)
                row += BLOCK
    for copy in copies:
        copy.wait()


def stacked_of(queries, block_pattern, steps, count):
    tok_dev, width = queries.shape
    blocks_dev, heads = tok_dev // BLOCK, width // HEAD_SIZE
    return pl.pallas_call(
        functools.partial(stack_kernel, steps, count),
        out_shape=[
            held((blocks_dev, heads * BLOCK, HEAD_SIZE)),
            held((blocks_dev, len(steps) * tok_dev, BLOCK)),
        ],
        in_specs=[HBM] * 2,
        out_specs=[VMEM] * 2,
        scratch_shapes=[
            pltpu.SMEM(block_pattern.shape, jnp.int32),
            pltpu.SemaphoreType.DMA(()),
            pltpu.SemaphoreType.DMA((blocks_dev, heads)),
        ],
        compiler_params=params(8),
        cost_estimate=cost(0, 1 << 20),
    )(in_hbm(queries), in_hbm(block_pattern))


def weights_kernel(q_ref, mask_ref, *refs):
    *key_refs, out_ref = refs
    blocks_dev, rows, _ = q_ref.shape
    group = min(rows, 512)
    exponent_scale = math.log2(math.e) / math.sqrt(HEAD_SIZE)
    keys = jnp.concatenate([ref[...] for ref in key_refs], axis=0)
    lane = jnp.where(first_lane((group, BLOCK)), 1.0, 0.0).astype(jnp.bfloat16)
    for a in range(blocks_dev):
        wide_keys = jnp.concatenate([keys, mask_ref[a]], axis=1)
        for first in range(0, rows, group):
            wide = jnp.concatenate([q_ref[a, first : first + group, :], lane], axis=1)
            scores = lax.dot_general(
                wide, wide_keys, (((1,), (1,)), ((), ())), preferred_element_type=jnp.float32
            )
            top = jnp.max(scores, axis=1, keepdims=True)
            out_ref[a, first : first + group, :] = jnp.exp2(
                (scores - top) * exponent_scale
            ).astype(jnp.bfloat16)


def weights_of(stacked, mask, key_parts):
    blocks_dev, rows, _ = stacked.shape
    keys = mask.shape[1]
    return pl.pallas_call(
        weights_kernel,
        out_shape=held((blocks_dev, rows, keys)),
        in_specs=[VMEM] * (2 + len(key_parts)),
        out_specs=VMEM,
        compiler_params=params(8 + (min(rows, 512) * keys * 16 >> 20)),
        cost_estimate=cost(400 * blocks_dev * rows * keys * HEAD_SIZE, 4 << 20),
    )(stacked, mask, *key_parts)


def values_kernel(count, weights_ref, *refs):
    values = jnp.concatenate([ref[...] for ref in refs[:count]], axis=0)
    values = jnp.concatenate([values, jnp.ones_like(values)], axis=1)
    piece_refs = refs[count:]
    blocks_dev, rows, _ = weights_ref.shape
    heads = rows // BLOCK
    pieces = len(piece_refs)
    group = heads // pieces
    for piece in range(pieces):
        for a in range(blocks_dev):
            first = piece * group
            summed = jnp.dot(
                weights_ref[a, first * BLOCK : (first + group) * BLOCK, :],
                values,
                preferred_element_type=jnp.float32,
            )
            result = (summed[:, :HEAD_SIZE] / summed[:, HEAD_SIZE:]).astype(jnp.bfloat16)
            for i in range(group):
                part = result[i * BLOCK : (i + 1) * BLOCK]
                tokens = slice(a * BLOCK, (a + 1) * BLOCK)
                column = i * HEAD_SIZE
                piece_refs[piece][tokens, column : column + HEAD_SIZE] = part


def attended_of(weights, value_parts, pieces):
    blocks_dev, rows, keys = weights.shape
    tokens, width = blocks_dev * BLOCK, rows // BLOCK * HEAD_SIZE
    shapes = [held((tokens, width // pieces))] * pieces
    return pl.pallas_call(
        functools.partial(values_kernel, len(value_parts)),
        out_shape=shapes,
        in_specs=[VMEM] * (1 + len(value_parts)),
        out_specs=[VMEM] * len(shapes),
        compiler_params=params(16),
        cost_estimate=cost(400 * tokens * width * keys, 1 << 20),
    )(weights, *value_parts)


def projection_kernel(places, width, fresh, last, weight_ref, *refs):
    refs = list(refs)
    total_ref = None if fresh else refs.pop(0)
    parts = refs[: len(places)]
    out_ref = refs[len(places)]
    columns = weight_ref.shape[1]
    tile = columns // 4 if last else columns
    me = lax.axis_index("head")
    copies = []
    for n in range(0, columns, tile):
        total = None if fresh else total_ref[:, n : n + tile]
        for (bits, offset), part in zip(places, parts):
            depth = part.shape[1]
            row = pl.multiple_of((me ^ bits) * width + offset, depth)
            term = jnp.dot(
                part[...],
                weight_ref[pl.ds(row, depth), n : n + tile],
                preferred_element_type=jnp.float32,
            )
            total = term if total is None else total + term
        if last:
            held_ref, sems = refs[len(places) + 1 :]
            held_ref[:, n : n + tile] = total.astype(held_ref.dtype)
            copy = pltpu.make_async_copy(
                held_ref.at[:, pl.ds(n, tile)], out_ref.at[:, pl.ds(n, tile)], sems.at[n // tile]
            )
            copy.start()
            copies.append(copy)
        else:
            out_ref[...] = total
    for copy in copies:
        copy.wait()


def projected(total, weight, width, places, parts, last=False):
    rows = parts[0].shape[0]
    columns = weight.shape[1]
    fresh = total is None
    operands = ([] if fresh else [total]) + parts
    shape = (rows, columns)
    depth = sum(part.shape[1] for part in parts)
    return pl.pallas_call(
        functools.partial(projection_kernel, places, width, fresh, last),
        out_shape=jax.ShapeDtypeStruct(shape, jnp.bfloat16) if last else held(shape, jnp.float32),
        in_specs=[VMEM] * (1 + len(operands)),
        out_specs=HBM if last else VMEM,
        scratch_shapes=[pltpu.VMEM(shape, jnp.bfloat16), pltpu.SemaphoreType.DMA((4,))]
        if last
        else [],
        compiler_params=params(8),
        cost_estimate=cost(8 * rows * depth * columns, 1 << 20),
    )(weight, *operands)


def gathered_over_ctx(part, steps):
    if len(steps) == 4:
        return [part] + [shifted(part, "ctx", step) for step in steps[1:]]
    whole = lax.all_gather(part, "ctx")
    return [whole[i] for i in range(len(steps))]


def on_device(queries, key_vectors, value_head_vectors, block_pattern, out_weight):
    heads_dev = queries.shape[1] // HEAD_SIZE
    count = lax.axis_size("ctx")
    steps = (0, 2, 1, 3) if count == 4 else tuple(range(count))
    barrier = lax.optimization_barrier
    keys, values = own_slices(key_vectors, value_head_vectors, queries.shape[1])
    key_parts = gathered_over_ctx(keys, steps)
    value_parts = gathered_over_ctx(values, steps)
    if count == 4:
        key_parts[2], queries = barrier((key_parts[2], queries))
    stacked, mask = stacked_of(queries, block_pattern, steps, count if count == 4 else None)
    weights = weights_of(stacked, mask, key_parts)
    if lax.axis_size("head") != 8:
        (att,) = attended_of(weights, value_parts, 1)
        mixed = jnp.dot(
            lax.all_gather(att, "head", axis=1, tiled=True),
            out_weight,
            preferred_element_type=jnp.float32,
        )
        return mixed.astype(jnp.bfloat16)

    barrier = lax.optimization_barrier
    weight = pltpu.with_memory_space_constraint(out_weight, pltpu.VMEM)
    a, b = attended_of(weights, value_parts, 2)
    xa = swapped(a, "head", 2)
    yb = swapped(b, "head", 4)
    xb = swapped(b, "head", 2)
    ya = swapped(a, "head", 4)
    sa = swapped(a, "head", 1)
    sb = swapped(b, "head", 1)
    width, half = heads_dev * HEAD_SIZE, heads_dev * HEAD_SIZE // 2
    mixed = projected(
        None, weight, width, ((0, 0), (0, half), (1, 0), (1, half)), [a, b, sa, sb]
    )
    xa, mixed = barrier((xa, mixed))
    da = swapped(xa, "head", 4)
    yb, mixed = barrier((yb, mixed))
    db = swapped(yb, "head", 2)
    xas, ybs = swapped(xa, "head", 1), swapped(yb, "head", 1)
    mixed = projected(
        mixed, weight, width, ((2, 0), (3, 0), (4, half), (5, half)), [xa, xas, yb, ybs]
    )
    xbs, yas = swapped(xb, "head", 1), swapped(ya, "head", 1)
    mixed = projected(
        mixed, weight, width, ((2, half), (3, half), (4, 0), (5, 0)), [xb, xbs, ya, yas]
    )
    da, mixed = barrier((da, mixed))
    das, dbs = swapped(da, "head", 1), swapped(db, "head", 1)
    mixed = projected(mixed, weight, width, ((6, 0), (6, half)), [da, db])
    return projected(mixed, weight, width, ((7, 0), (7, half)), [das, dbs], True)


def solution(mesh):
    return jax.shard_map(
        on_device,
        mesh=mesh,
        in_specs=(P("ctx", "head"), P("ctx", None), P("ctx", None), P(), P(None, "head")),
        out_specs=P("ctx", "head"),
        check_vma=False,
    )
```

```python
import functools
import math

import jax
import jax.numpy as jnp
from jax import lax
from jax.experimental import pallas as pl
from jax.experimental.pallas import tpu as pltpu
from jax.sharding import PartitionSpec as P

QUERY_HEADS = 64
KEY_VALUE_HEADS = 8
HEAD_SIZE = 128
BLOCK = 128
FAR = -1e30

SMEM = pl.BlockSpec(memory_space=pltpu.SMEM)
VMEM = pl.BlockSpec(memory_space=pltpu.VMEM)
HBM = pl.BlockSpec(memory_space=pltpu.HBM)


def params(mib):
    return pltpu.CompilerParams(vmem_limit_bytes=mib << 20)


def held(shape, dtype=jnp.bfloat16):
    return pltpu.VMEM(shape, dtype)


def in_hbm(value):
    return pltpu.with_memory_space_constraint(value, pltpu.HBM)


def cost(flops, moved):
    return pl.CostEstimate(flops=flops, bytes_accessed=moved, transcendentals=0)


def shifted(value, axis, steps):
    count = lax.axis_size(axis)
    return lax.ppermute(value, axis, [(source, (source + steps) % count) for source in range(count)])


def swapped(value, axis, bits):
    count = lax.axis_size(axis)
    return lax.ppermute(value, axis, [(source, source ^ bits) for source in range(count)])


def first_lane(shape):
    return lax.broadcasted_iota(jnp.int32, shape, 1) == 0


def slice_kernel(width, keys_ref, values_ref, own_keys_ref, own_values_ref, sems):
    heads = width // HEAD_SIZE
    head = lax.div(lax.axis_index("head") * heads, QUERY_HEADS // KEY_VALUE_HEADS)
    columns = pl.ds(pl.multiple_of(head * HEAD_SIZE, HEAD_SIZE), HEAD_SIZE)
    copies = [
        pltpu.make_async_copy(keys_ref.at[:, columns], own_keys_ref, sems.at[0]),
        pltpu.make_async_copy(values_ref.at[:, columns], own_values_ref, sems.at[1]),
    ]
    for copy in copies:
        copy.start()
    for copy in copies:
        copy.wait()


def own_slices(key_vectors, value_vectors, width):
    own = held((key_vectors.shape[0], HEAD_SIZE))
    return pl.pallas_call(
        functools.partial(slice_kernel, width),
        out_shape=[own, own],
        in_specs=[HBM] * 2,
        out_specs=[VMEM] * 2,
        scratch_shapes=[pltpu.SemaphoreType.DMA((2,))],
        compiler_params=params(8),
        cost_estimate=cost(0, 1 << 18),
    )(in_hbm(key_vectors), in_hbm(value_vectors))


def stack_kernel(steps, count, q_ref, pattern_ref, *refs):
    stacked_ref, mask_ref, table_ref, table_sem, sems = refs
    blocks_dev, rows, _ = stacked_ref.shape
    heads = rows // BLOCK
    table = pltpu.make_async_copy(pattern_ref, table_ref, table_sem)
    table.start()
    copies = []
    for a in range(blocks_dev):
        for h in range(heads):
            copies.append(
                pltpu.make_async_copy(
                    q_ref.at[pl.ds(a * BLOCK, BLOCK), pl.ds(h * HEAD_SIZE, HEAD_SIZE)],
                    stacked_ref.at[a, pl.ds(h * BLOCK, BLOCK)],
                    sems.at[a, h],
                )
            )
    for copy in copies:
        copy.start()
    table.wait()
    me = lax.axis_index("ctx")
    lane = first_lane((BLOCK, BLOCK))
    for a in range(blocks_dev):
        query_block = me * blocks_dev + a
        row = 0
        for step in steps:
            source = step if count is None else lax.rem(me + (count - step), count)
            for j in range(blocks_dev):
                key_block = source * blocks_dev + j
                on = (table_ref[query_block, key_block] == 1) | (query_block == key_block)
                mask_ref[a, row : row + BLOCK, :] = jnp.where(
                    lane, jnp.where(on, 0.0, FAR), 0.0
                ).astype(jnp.bfloat16)
                row += BLOCK
    for copy in copies:
        copy.wait()


def stacked_of(queries, block_pattern, steps, count):
    tok_dev, width = queries.shape
    blocks_dev, heads = tok_dev // BLOCK, width // HEAD_SIZE
    return pl.pallas_call(
        functools.partial(stack_kernel, steps, count),
        out_shape=[
            held((blocks_dev, heads * BLOCK, HEAD_SIZE)),
            held((blocks_dev, len(steps) * tok_dev, BLOCK)),
        ],
        in_specs=[HBM] * 2,
        out_specs=[VMEM] * 2,
        scratch_shapes=[
            pltpu.SMEM(block_pattern.shape, jnp.int32),
            pltpu.SemaphoreType.DMA(()),
            pltpu.SemaphoreType.DMA((blocks_dev, heads)),
        ],
        compiler_params=params(8),
        cost_estimate=cost(0, 1 << 20),
    )(in_hbm(queries), in_hbm(block_pattern))


def weights_kernel(q_ref, mask_ref, *refs):
    *key_refs, out_ref = refs
    blocks_dev, rows, _ = q_ref.shape
    group = min(rows, 512)
    exponent_scale = math.log2(math.e) / math.sqrt(HEAD_SIZE)
    keys = jnp.concatenate([ref[...] for ref in key_refs], axis=0)
    lane = jnp.where(first_lane((group, BLOCK)), 1.0, 0.0).astype(jnp.bfloat16)
    for a in range(blocks_dev):
        wide_keys = jnp.concatenate([keys, mask_ref[a]], axis=1)
        for first in range(0, rows, group):
            wide = jnp.concatenate([q_ref[a, first : first + group, :], lane], axis=1)
            scores = lax.dot_general(
                wide, wide_keys, (((1,), (1,)), ((), ())), preferred_element_type=jnp.float32
            )
            top = jnp.max(scores, axis=1, keepdims=True)
            out_ref[a, first : first + group, :] = jnp.exp2(
                (scores - top) * exponent_scale
            ).astype(jnp.bfloat16)


def weights_of(stacked, mask, key_parts):
    blocks_dev, rows, _ = stacked.shape
    keys = mask.shape[1]
    return pl.pallas_call(
        weights_kernel,
        out_shape=held((blocks_dev, rows, keys)),
        in_specs=[VMEM] * (2 + len(key_parts)),
        out_specs=VMEM,
        compiler_params=params(8 + (min(rows, 512) * keys * 16 >> 20)),
        cost_estimate=cost(400 * blocks_dev * rows * keys * HEAD_SIZE, 4 << 20),
    )(stacked, mask, *key_parts)


def values_kernel(count, weights_ref, *refs):
    values = jnp.concatenate([ref[...] for ref in refs[:count]], axis=0)
    values = jnp.concatenate([values, jnp.ones_like(values)], axis=1)
    piece_refs = refs[count:]
    blocks_dev, rows, _ = weights_ref.shape
    heads = rows // BLOCK
    pieces = len(piece_refs)
    group = heads // pieces
    for piece in range(pieces):
        for a in range(blocks_dev):
            first = piece * group
            summed = jnp.dot(
                weights_ref[a, first * BLOCK : (first + group) * BLOCK, :],
                values,
                preferred_element_type=jnp.float32,
            )
            result = (summed[:, :HEAD_SIZE] / summed[:, HEAD_SIZE:]).astype(jnp.bfloat16)
            for i in range(group):
                part = result[i * BLOCK : (i + 1) * BLOCK]
                tokens = slice(a * BLOCK, (a + 1) * BLOCK)
                column = i * HEAD_SIZE
                piece_refs[piece][tokens, column : column + HEAD_SIZE] = part


def attended_of(weights, value_parts, pieces):
    blocks_dev, rows, keys = weights.shape
    tokens, width = blocks_dev * BLOCK, rows // BLOCK * HEAD_SIZE
    shapes = [held((tokens, width // pieces))] * pieces
    return pl.pallas_call(
        functools.partial(values_kernel, len(value_parts)),
        out_shape=shapes,
        in_specs=[VMEM] * (1 + len(value_parts)),
        out_specs=[VMEM] * len(shapes),
        compiler_params=params(16),
        cost_estimate=cost(400 * tokens * width * keys, 1 << 20),
    )(weights, *value_parts)


def projection_kernel(places, width, fresh, last, weight_ref, *refs):
    refs = list(refs)
    total_ref = None if fresh else refs.pop(0)
    parts = refs[: len(places)]
    out_ref = refs[len(places)]
    columns = weight_ref.shape[1]
    tile = columns // 4 if last else columns
    me = lax.axis_index("head")
    copies = []
    for n in range(0, columns, tile):
        total = None if fresh else total_ref[:, n : n + tile]
        for (bits, offset), part in zip(places, parts):
            depth = part.shape[1]
            row = pl.multiple_of((me ^ bits) * width + offset, depth)
            term = jnp.dot(
                part[...],
                weight_ref[pl.ds(row, depth), n : n + tile],
                preferred_element_type=jnp.float32,
            )
            total = term if total is None else total + term
        if last:
            held_ref, sems = refs[len(places) + 1 :]
            held_ref[:, n : n + tile] = total.astype(held_ref.dtype)
            copy = pltpu.make_async_copy(
                held_ref.at[:, pl.ds(n, tile)], out_ref.at[:, pl.ds(n, tile)], sems.at[n // tile]
            )
            copy.start()
            copies.append(copy)
        else:
            out_ref[...] = total
    for copy in copies:
        copy.wait()


def projected(total, weight, width, places, parts, last=False):
    rows = parts[0].shape[0]
    columns = weight.shape[1]
    fresh = total is None
    operands = ([] if fresh else [total]) + parts
    shape = (rows, columns)
    depth = sum(part.shape[1] for part in parts)
    return pl.pallas_call(
        functools.partial(projection_kernel, places, width, fresh, last),
        out_shape=jax.ShapeDtypeStruct(shape, jnp.bfloat16) if last else held(shape, jnp.float32),
        in_specs=[VMEM] * (1 + len(operands)),
        out_specs=HBM if last else VMEM,
        scratch_shapes=[pltpu.VMEM(shape, jnp.bfloat16), pltpu.SemaphoreType.DMA((4,))]
        if last
        else [],
        compiler_params=params(8),
        cost_estimate=cost(8 * rows * depth * columns, 1 << 20),
    )(weight, *operands)


def gathered_over_ctx(part, steps):
    if len(steps) == 4:
        return [part] + [shifted(part, "ctx", step) for step in steps[1:]]
    whole = lax.all_gather(part, "ctx")
    return [whole[i] for i in range(len(steps))]


def on_device(queries, key_vectors, value_head_vectors, block_pattern, out_weight):
    heads_dev = queries.shape[1] // HEAD_SIZE
    count = lax.axis_size("ctx")
    steps = (0, 2, 1, 3) if count == 4 else tuple(range(count))
    barrier = lax.optimization_barrier
    keys, values = own_slices(key_vectors, value_head_vectors, queries.shape[1])
    key_parts = gathered_over_ctx(keys, steps)
    value_parts = gathered_over_ctx(values, steps)
    if count == 4:
        key_parts[2], queries = barrier((key_parts[2], queries))
    stacked, mask = stacked_of(queries, block_pattern, steps, count if count == 4 else None)
    weights = weights_of(stacked, mask, key_parts)
    if lax.axis_size("head") != 8:
        (att,) = attended_of(weights, value_parts, 1)
        mixed = jnp.dot(
            lax.all_gather(att, "head", axis=1, tiled=True),
            out_weight,
            preferred_element_type=jnp.float32,
        )
        return mixed.astype(jnp.bfloat16)

    barrier = lax.optimization_barrier
    weight = pltpu.with_memory_space_constraint(out_weight, pltpu.VMEM)
    a, b = attended_of(weights, value_parts, 2)
    xa = swapped(a, "head", 2)
    yb = swapped(b, "head", 4)
    xb = swapped(b, "head", 2)
    ya = swapped(a, "head", 4)
    sa = swapped(a, "head", 1)
    sb = swapped(b, "head", 1)
    width, half = heads_dev * HEAD_SIZE, heads_dev * HEAD_SIZE // 2
    mixed = projected(
        None, weight, width, ((0, 0), (0, half), (1, 0)), [a, b, sa]
    )
    xa, mixed = barrier((xa, mixed))
    da = swapped(xa, "head", 4)
    yb, mixed = barrier((yb, mixed))
    db = swapped(yb, "head", 2)
    xas, ybs = swapped(xa, "head", 1), swapped(yb, "head", 1)
    mixed = projected(
        mixed, weight, width, ((2, 0), (3, 0), (4, half), (5, half), (1, half)), [xa, xas, yb, ybs, sb]
    )
    xbs, yas = swapped(xb, "head", 1), swapped(ya, "head", 1)
    mixed = projected(
        mixed, weight, width, ((2, half), (3, half), (4, 0), (5, 0)), [xb, xbs, ya, yas]
    )
    da, mixed = barrier((da, mixed))
    das, dbs = swapped(da, "head", 1), swapped(db, "head", 1)
    mixed = projected(mixed, weight, width, ((6, 0), (6, half)), [da, db])
    return projected(mixed, weight, width, ((7, 0), (7, half)), [das, dbs], True)


def solution(mesh):
    return jax.shard_map(
        on_device,
        mesh=mesh,
        in_specs=(P("ctx", "head"), P("ctx", None), P("ctx", None), P(), P(None, "head")),
        out_specs=P("ctx", "head"),
        check_vma=False,
    )
```

```python
import functools
import math

import jax
import jax.numpy as jnp
from jax import lax
from jax.experimental import pallas as pl
from jax.experimental.pallas import tpu as pltpu
from jax.sharding import PartitionSpec as P

QUERY_HEADS = 64
KEY_VALUE_HEADS = 8
HEAD_SIZE = 128
BLOCK = 128
FAR = -1e30

SMEM = pl.BlockSpec(memory_space=pltpu.SMEM)
VMEM = pl.BlockSpec(memory_space=pltpu.VMEM)
HBM = pl.BlockSpec(memory_space=pltpu.HBM)


def params(mib):
    return pltpu.CompilerParams(vmem_limit_bytes=mib << 20)


def held(shape, dtype=jnp.bfloat16):
    return pltpu.VMEM(shape, dtype)


def in_hbm(value):
    return pltpu.with_memory_space_constraint(value, pltpu.HBM)


def cost(flops, moved):
    return pl.CostEstimate(flops=flops, bytes_accessed=moved, transcendentals=0)


def shifted(value, axis, steps):
    count = lax.axis_size(axis)
    return lax.ppermute(value, axis, [(source, (source + steps) % count) for source in range(count)])


def swapped(value, axis, bits):
    count = lax.axis_size(axis)
    return lax.ppermute(value, axis, [(source, source ^ bits) for source in range(count)])


def first_lane(shape):
    return lax.broadcasted_iota(jnp.int32, shape, 1) == 0


def slice_kernel(width, keys_ref, values_ref, own_keys_ref, own_values_ref, sems):
    heads = width // HEAD_SIZE
    head = lax.div(lax.axis_index("head") * heads, QUERY_HEADS // KEY_VALUE_HEADS)
    columns = pl.ds(pl.multiple_of(head * HEAD_SIZE, HEAD_SIZE), HEAD_SIZE)
    copies = [
        pltpu.make_async_copy(keys_ref.at[:, columns], own_keys_ref, sems.at[0]),
        pltpu.make_async_copy(values_ref.at[:, columns], own_values_ref, sems.at[1]),
    ]
    for copy in copies:
        copy.start()
    for copy in copies:
        copy.wait()


def own_slices(key_vectors, value_vectors, width):
    own = held((key_vectors.shape[0], HEAD_SIZE))
    return pl.pallas_call(
        functools.partial(slice_kernel, width),
        out_shape=[own, own],
        in_specs=[HBM] * 2,
        out_specs=[VMEM] * 2,
        scratch_shapes=[pltpu.SemaphoreType.DMA((2,))],
        compiler_params=params(8),
        cost_estimate=cost(0, 1 << 18),
    )(in_hbm(key_vectors), in_hbm(value_vectors))


def stack_kernel(steps, count, q_ref, pattern_ref, *refs):
    stacked_ref, mask_ref, table_ref, table_sem, sems = refs
    blocks_dev, rows, _ = stacked_ref.shape
    heads = rows // BLOCK
    table = pltpu.make_async_copy(pattern_ref, table_ref, table_sem)
    table.start()
    copies = []
    for a in range(blocks_dev):
        for h in range(heads):
            copies.append(
                pltpu.make_async_copy(
                    q_ref.at[pl.ds(a * BLOCK, BLOCK), pl.ds(h * HEAD_SIZE, HEAD_SIZE)],
                    stacked_ref.at[a, pl.ds(h * BLOCK, BLOCK)],
                    sems.at[a, h],
                )
            )
    for copy in copies:
        copy.start()
    table.wait()
    me = lax.axis_index("ctx")
    lane = first_lane((BLOCK, BLOCK))
    for a in range(blocks_dev):
        query_block = me * blocks_dev + a
        row = 0
        for step in steps:
            source = step if count is None else lax.rem(me + (count - step), count)
            for j in range(blocks_dev):
                key_block = source * blocks_dev + j
                on = (table_ref[query_block, key_block] == 1) | (query_block == key_block)
                mask_ref[a, row : row + BLOCK, :] = jnp.where(
                    lane, jnp.where(on, 0.0, FAR), 0.0
                ).astype(jnp.bfloat16)
                row += BLOCK
    for copy in copies:
        copy.wait()


def stacked_of(queries, block_pattern, steps, count):
    tok_dev, width = queries.shape
    blocks_dev, heads = tok_dev // BLOCK, width // HEAD_SIZE
    return pl.pallas_call(
        functools.partial(stack_kernel, steps, count),
        out_shape=[
            held((blocks_dev, heads * BLOCK, HEAD_SIZE)),
            held((blocks_dev, len(steps) * tok_dev, BLOCK)),
        ],
        in_specs=[HBM] * 2,
        out_specs=[VMEM] * 2,
        scratch_shapes=[
            pltpu.SMEM(block_pattern.shape, jnp.int32),
            pltpu.SemaphoreType.DMA(()),
            pltpu.SemaphoreType.DMA((blocks_dev, heads)),
        ],
        compiler_params=params(8),
        cost_estimate=cost(0, 1 << 20),
    )(in_hbm(queries), in_hbm(block_pattern))


def weights_kernel(q_ref, mask_ref, *refs):
    *key_refs, out_ref = refs
    blocks_dev, rows, _ = q_ref.shape
    group = min(rows, 512)
    exponent_scale = math.log2(math.e) / math.sqrt(HEAD_SIZE)
    keys = jnp.concatenate([ref[...] for ref in key_refs], axis=0)
    lane = jnp.where(first_lane((group, BLOCK)), 1.0, 0.0).astype(jnp.bfloat16)
    for a in range(blocks_dev):
        wide_keys = jnp.concatenate([keys, mask_ref[a]], axis=1)
        for first in range(0, rows, group):
            wide = jnp.concatenate([q_ref[a, first : first + group, :], lane], axis=1)
            scores = lax.dot_general(
                wide, wide_keys, (((1,), (1,)), ((), ())), preferred_element_type=jnp.float32
            )
            top = jnp.max(scores, axis=1, keepdims=True)
            out_ref[a, first : first + group, :] = jnp.exp2(
                (scores - top) * exponent_scale
            ).astype(jnp.bfloat16)


def weights_of(stacked, mask, key_parts):
    blocks_dev, rows, _ = stacked.shape
    keys = mask.shape[1]
    return pl.pallas_call(
        weights_kernel,
        out_shape=held((blocks_dev, rows, keys)),
        in_specs=[VMEM] * (2 + len(key_parts)),
        out_specs=VMEM,
        compiler_params=params(8 + (min(rows, 512) * keys * 16 >> 20)),
        cost_estimate=cost(400 * blocks_dev * rows * keys * HEAD_SIZE, 4 << 20),
    )(stacked, mask, *key_parts)


def values_kernel(count, weights_ref, *refs):
    values = jnp.concatenate([ref[...] for ref in refs[:count]], axis=0)
    values = jnp.concatenate([values, jnp.ones_like(values)], axis=1)
    piece_refs = refs[count:]
    blocks_dev, rows, _ = weights_ref.shape
    heads = rows // BLOCK
    pieces = len(piece_refs)
    group = heads // pieces
    for piece in range(pieces):
        for a in range(blocks_dev):
            first = piece * group
            summed = jnp.dot(
                weights_ref[a, first * BLOCK : (first + group) * BLOCK, :],
                values,
                preferred_element_type=jnp.float32,
            )
            result = (summed[:, :HEAD_SIZE] / summed[:, HEAD_SIZE:]).astype(jnp.bfloat16)
            for i in range(group):
                part = result[i * BLOCK : (i + 1) * BLOCK]
                tokens = slice(a * BLOCK, (a + 1) * BLOCK)
                column = i * HEAD_SIZE
                piece_refs[piece][tokens, column : column + HEAD_SIZE] = part


def attended_of(weights, value_parts, pieces):
    blocks_dev, rows, keys = weights.shape
    tokens, width = blocks_dev * BLOCK, rows // BLOCK * HEAD_SIZE
    shapes = [held((tokens, width // pieces))] * pieces
    return pl.pallas_call(
        functools.partial(values_kernel, len(value_parts)),
        out_shape=shapes,
        in_specs=[VMEM] * (1 + len(value_parts)),
        out_specs=[VMEM] * len(shapes),
        compiler_params=params(16),
        cost_estimate=cost(400 * tokens * width * keys, 1 << 20),
    )(weights, *value_parts)


def projection_kernel(places, width, fresh, last, weight_ref, *refs):
    refs = list(refs)
    total_ref = None if fresh else refs.pop(0)
    parts = refs[: len(places)]
    out_ref = refs[len(places)]
    columns = weight_ref.shape[1]
    tile = columns // 2 if last else columns
    me = lax.axis_index("head")
    copies = []
    for n in range(0, columns, tile):
        total = None if fresh else total_ref[:, n : n + tile]
        for (bits, offset), part in zip(places, parts):
            depth = part.shape[1]
            row = pl.multiple_of((me ^ bits) * width + offset, depth)
            term = jnp.dot(
                part[...],
                weight_ref[pl.ds(row, depth), n : n + tile],
                preferred_element_type=jnp.float32,
            )
            total = term if total is None else total + term
        if last:
            held_ref, sems = refs[len(places) + 1 :]
            held_ref[:, n : n + tile] = total.astype(held_ref.dtype)
            copy = pltpu.make_async_copy(
                held_ref.at[:, pl.ds(n, tile)], out_ref.at[:, pl.ds(n, tile)], sems.at[n // tile]
            )
            copy.start()
            copies.append(copy)
        else:
            out_ref[...] = total
    for copy in copies:
        copy.wait()


def projected(total, weight, width, places, parts, last=False):
    rows = parts[0].shape[0]
    columns = weight.shape[1]
    fresh = total is None
    operands = ([] if fresh else [total]) + parts
    shape = (rows, columns)
    depth = sum(part.shape[1] for part in parts)
    return pl.pallas_call(
        functools.partial(projection_kernel, places, width, fresh, last),
        out_shape=jax.ShapeDtypeStruct(shape, jnp.bfloat16) if last else held(shape, jnp.float32),
        in_specs=[VMEM] * (1 + len(operands)),
        out_specs=HBM if last else VMEM,
        scratch_shapes=[pltpu.VMEM(shape, jnp.bfloat16), pltpu.SemaphoreType.DMA((4,))]
        if last
        else [],
        compiler_params=params(8),
        cost_estimate=cost(8 * rows * depth * columns, 1 << 20),
    )(weight, *operands)


def gathered_over_ctx(part, steps):
    if len(steps) == 4:
        return [part] + [shifted(part, "ctx", step) for step in steps[1:]]
    whole = lax.all_gather(part, "ctx")
    return [whole[i] for i in range(len(steps))]


def on_device(queries, key_vectors, value_head_vectors, block_pattern, out_weight):
    heads_dev = queries.shape[1] // HEAD_SIZE
    count = lax.axis_size("ctx")
    steps = (0, 2, 1, 3) if count == 4 else tuple(range(count))
    barrier = lax.optimization_barrier
    keys, values = own_slices(key_vectors, value_head_vectors, queries.shape[1])
    key_parts = gathered_over_ctx(keys, steps)
    value_parts = gathered_over_ctx(values, steps)
    if count == 4:
        key_parts[2], queries = barrier((key_parts[2], queries))
    stacked, mask = stacked_of(queries, block_pattern, steps, count if count == 4 else None)
    weights = weights_of(stacked, mask, key_parts)
    if lax.axis_size("head") != 8:
        (att,) = attended_of(weights, value_parts, 1)
        mixed = jnp.dot(
            lax.all_gather(att, "head", axis=1, tiled=True),
            out_weight,
            preferred_element_type=jnp.float32,
        )
        return mixed.astype(jnp.bfloat16)

    barrier = lax.optimization_barrier
    weight = pltpu.with_memory_space_constraint(out_weight, pltpu.VMEM)
    a, b = attended_of(weights, value_parts, 2)
    xa = swapped(a, "head", 2)
    yb = swapped(b, "head", 4)
    xb = swapped(b, "head", 2)
    ya = swapped(a, "head", 4)
    sa = swapped(a, "head", 1)
    sb = swapped(b, "head", 1)
    width, half = heads_dev * HEAD_SIZE, heads_dev * HEAD_SIZE // 2
    mixed = projected(
        None, weight, width, ((0, 0), (0, half), (1, 0), (1, half)), [a, b, sa, sb]
    )
    xa, mixed = barrier((xa, mixed))
    da = swapped(xa, "head", 4)
    yb, mixed = barrier((yb, mixed))
    db = swapped(yb, "head", 2)
    xas, ybs = swapped(xa, "head", 1), swapped(yb, "head", 1)
    mixed = projected(
        mixed, weight, width, ((2, 0), (3, 0), (4, half), (5, half)), [xa, xas, yb, ybs]
    )
    xbs, yas = swapped(xb, "head", 1), swapped(ya, "head", 1)
    mixed = projected(
        mixed, weight, width, ((2, half), (3, half), (4, 0), (5, 0)), [xb, xbs, ya, yas]
    )
    da, mixed = barrier((da, mixed))
    das, dbs = swapped(da, "head", 1), swapped(db, "head", 1)
    mixed = projected(mixed, weight, width, ((6, 0), (6, half)), [da, db])
    return projected(mixed, weight, width, ((7, 0), (7, half)), [das, dbs], True)


def solution(mesh):
    return jax.shard_map(
        on_device,
        mesh=mesh,
        in_specs=(P("ctx", "head"), P("ctx", None), P("ctx", None), P(), P(None, "head")),
        out_specs=P("ctx", "head"),
        check_vma=False,
    )
```
